32 devices in a mesh: ctx: 8 (over z, y), head: 4 (over x, core).
Axes of the slice: x: 2, y: 2, z: 4, core: 2. Of those that a mesh axis runs over, the one named last changes fastest.
Arguments:
- query: bfloat16 [1024, 8192], P('ctx', 'head'), may hold values from -240 to 240
- keys: bfloat16 [1024, 8192], P('ctx', 'head'), may hold values from -4 to 4
- values: bfloat16 [1024, 8192], P('ctx', 'head'), may hold values from -6 to 6
- memory_keys: bfloat16 [768, 8192], P('ctx', 'head'), may hold values from -6 to 6
- memory_values: bfloat16 [768, 8192], P('ctx', 'head'), may hold values from -6 to 6
- routes: int32 [96, 1], replicated, may hold values from 0 to 7; in each aligned block of 12 rows (0 to 11, 12 to 23, ...) at most 2 rows name the same one
- documents: int32 [1024], replicated, may hold values from 0 to 15, never falling along the last dimension, each value on 1 to 257 neighbouring positions
- cotangent: bfloat16 [1024, 8192], P('ctx', 'head'), may hold values from -40 to 40
Outputs:
- attended: bfloat16 [1024, 8192], P('ctx', 'head')
- query_grad: bfloat16 [1024, 8192], P('ctx', 'head')
- key_grad: bfloat16 [1024, 8192], P('ctx', 'head')
- value_grad: bfloat16 [1024, 8192], P('ctx', 'head')
The draws below stay inside these ranges and needn't reach their ends.
Inputs may be any that keep to these rules, and one draw needn't show every extreme that they name: `routes`: in the 12 aligned rows of one segment block's store, no segment block is named more than 2 times. `documents`: document numbers never fall; a document covers 1 to 257 positions.
All inputs are finite; a program needn't handle non-finite values.
Results may differ from the reference program's by a relative error of at most 0.01.
Values may be sent and summed in bfloat16 or wider, within the bound.
No kernel may reach another device: no remote copies, remote signals or barrier semaphores. Data moves between devices by JAX's collectives and lax.ppermute only.
A program may use at most 64 MiB of HBM per device.

```python
import math
import jax
import jax.numpy as jnp
import numpy as np
from jax import lax

HEADS = 64
HDIM = 128
TOK_DEV = 128
BLK = 8
CAP = 2
MB_DEV = 12
REACH = 3
TOKENS = 1024
MEM_BLOCKS = 96
MEM_ROWS = 768
DOC_MAX = 257
DOCS = 16
N_CTX = 8


def shared_base(key):
    base = jax.random.normal(jax.random.fold_in(key, 11), (TOKENS, HEADS * HDIM), jnp.float32)
    return jnp.clip(base, -4.0, 4.0)


def draw_keys(key, part):
    base = shared_base(key)
    return base.astype(jnp.bfloat16)


def draw_query(key, part):
    own = jnp.clip(jax.random.normal(jax.random.fold_in(key, 12), (TOKENS, HEADS * HDIM), jnp.float32), -4.0, 4.0)
    return own.astype(jnp.bfloat16)


def draw_cotangent(key, part):
    width = HEADS * HDIM
    rows = jnp.arange(TOKENS, dtype=jnp.int32).astype(jnp.float32)
    heads = (jnp.arange(width, dtype=jnp.int32) // HDIM).astype(jnp.float32)
    rise_rows = 1.0 + 0.732 * rows / (TOKENS - 1)
    rise_cols = 1.0 + 0.732 * heads / (HEADS - 1)
    row_scale = jnp.power(10.0, jax.random.uniform(jax.random.fold_in(key, 21), (TOKENS,), jnp.float32))
    col_scale = jnp.power(10.0, jax.random.uniform(jax.random.fold_in(key, 22), (width,), jnp.float32))
    noise = jnp.clip(jax.random.normal(jax.random.fold_in(key, 23), (TOKENS, width), jnp.float32), -4.0, 4.0)
    result = 0.03 * noise * (row_scale * rise_rows)[:, None] * (col_scale * rise_cols)[None, :]
    return result.astype(jnp.bfloat16)


def shard_levels(rng, dims, cuts, least, largest):
    loudness, own = 1.0, jax.random.fold_in(rng, 6)
    for dim, shards_of in cuts:
        heights = jnp.exp(jax.random.uniform(jax.random.fold_in(own, dim), (shards_of,), jnp.float32, least / len(cuts), largest / len(cuts)))
        loudness = loudness * jnp.repeat(heights, dims[dim] // shards_of).reshape([-1 if axis == dim else 1 for axis in range(len(dims))])
    return loudness


def length_profile(number_of, total, reach, skew):
    weights = [(1 << 20) // math.isqrt(standing ** skew) + 1 for standing in range(2, number_of + 1)]
    spare, holding = total - reach - (number_of - 1), [1] * (number_of - 1)
    while spare > 0:
        free = [i for i in range(number_of - 1) if holding[i] < reach]
        mass, budget = sum([weights[i] for i in free]), spare
        for i in free:
            extra = min(reach - holding[i], max(1, budget * weights[i] // mass), spare)
            holding[i] = holding[i] + extra
            spare = spare - extra
    return np.array([reach] + holding)


def ragged_sizes(stream_key, amount, total, limit, lean):
    if amount == 2:
        one = jax.random.randint(stream_key, (), max(1, total - limit), min(limit, total - 1) + 1)
        return jnp.stack([one, total - one])
    sizes = jnp.asarray(length_profile(amount, total, limit, lean), jnp.int32)
    twos = (amount - 1) // 2
    giver, receiver = sizes[1:1 + 2 * twos:2], sizes[2:2 + 2 * twos:2]
    slack = jnp.minimum(giver - 1, limit - receiver)
    shifted = jax.random.randint(jax.random.fold_in(stream_key, 1), (twos,), 0, 1 << 20) % (slack + 1)
    sizes = sizes.at[1:1 + 2 * twos:2].set(giver - shifted).at[2:2 + 2 * twos:2].set(receiver + shifted)
    return sizes[jax.random.permutation(jax.random.fold_in(stream_key, 2), amount)]


def assign_block(rng, own, number, rows, count, top, reach, skew):
    sequence = jax.random.permutation(rng, count)
    heavy_load, usual = shares(count, rows * top, reach, skew, True), shares(count, rows * top, reach, skew, False)
    places = jnp.arange(count)

    def named(tallies, rotation):
        used = int((tallies > 0).sum())
        fixed = max(1, used // 4)
        shifted = fixed + (places - fixed + rotation * (used - fixed)) % max(1, count - fixed)
        return jnp.zeros((count,), jnp.int32).at[sequence[jnp.where(places < fixed, places, shifted)]].set(jnp.asarray(tallies, jnp.int32))

    tallies = jnp.where(number % 4 == 0, named(heavy_load, number // 4), named(usual, number - number // 4 - 1))
    mixed = jax.random.permutation(jax.random.fold_in(own, 3), count)
    source_of, receiver = mixed[0:count // 2 * 2:2], mixed[1:count // 2 * 2:2]
    room = jnp.minimum(tallies[source_of] - 1, reach - tallies[receiver]) // 2
    room = jnp.where((source_of == sequence[0]) | (receiver == sequence[0]) | (tallies[receiver] == 0), 0, jnp.maximum(room, 0))
    shifted = jax.random.randint(jax.random.fold_in(own, 4), (count // 2,), 0, 1 << 20) % (room + 1)
    tallies = tallies.at[source_of].add(-shifted).at[receiver].add(shifted)
    items = jnp.searchsorted(jnp.cumsum(tallies), jnp.arange(rows * top), side="right").astype(jnp.int32)
    grid = items.reshape(top, rows).T
    grid = grid[jax.random.permutation(jax.random.fold_in(own, 1), rows)]
    rotation = jax.random.randint(jax.random.fold_in(own, 2), (rows, 1), 0, top)
    return jnp.take_along_axis(grid, (jnp.arange(top)[None, :] + rotation) % top, axis=1)


def shares(count, total, limit, lean, full):
    loads = [(1 << 20) // math.isqrt(grade ** lean) + 1 for grade in range(1, count + 1)]
    largest = limit if full else min(limit, max(-(-total // count), total * loads[0] // sum(loads)))
    least = 1 if total - largest >= count - 1 else 0
    counts, rest = [largest] + [least] * (count - 1), total - largest - least * (count - 1)
    while rest > 0:
        candidates = [i for i in range(1, count) if counts[i] < largest] or [i for i in range(1, count) if counts[i] < limit]
        pool, left = sum([loads[i] for i in candidates]), rest
        for i in candidates:
            extra = min(limit - counts[i], max(1, left * loads[i] // pool), rest)
            counts[i] = counts[i] + extra
            rest = rest - extra
    return np.array(counts)


def centred(key, shape, deviation, reach, cuts=(), kind=jnp.bfloat16):
    values = jax.random.normal(key, shape, jnp.float32) * deviation
    if len(cuts) > 0:
        values = shard_levels(key, shape, cuts, -0.22, 0.18) * values
    return jnp.clip(values, min=-reach, max=reach).astype(kind)


def setup_inputs(seed: int = 0) -> dict:
    key_list = jax.random.split(jax.random.key(seed), 9)
    query = draw_query(jax.random.fold_in(key_list[8], 71), 0)
    keys = draw_keys(jax.random.fold_in(key_list[8], 71), 0)
    values = centred(key_list[2], (TOKENS, HEADS * HDIM), 1.0, 6.0, ((0, 8), (1, 4)))
    memory_keys = centred(key_list[3], (MEM_ROWS, HEADS * HDIM), 1.0, 6.0, ((0, 8), (1, 4)))
    memory_values = centred(key_list[4], (MEM_ROWS, HEADS * HDIM), 1.0, 6.0, ((0, 8), (1, 4)))
    routes_keys = jax.random.split(jax.random.fold_in(key_list[5], 1), MEM_BLOCKS // MB_DEV)
    routes_turns = jax.random.permutation(jax.random.fold_in(key_list[5], 3), MEM_BLOCKS // MB_DEV)
    routes = jax.vmap(lambda own, number: assign_block(jax.random.fold_in(key_list[5], 2), own, number, MB_DEV, N_CTX, 1, CAP, 2))(routes_keys, routes_turns).reshape((MEM_BLOCKS, 1))
    documents = jnp.searchsorted(jnp.cumsum(ragged_sizes(key_list[6], DOCS, TOKENS, DOC_MAX, 2)), jnp.arange(TOKENS), side="right").astype(jnp.int32)
    cotangent = draw_cotangent(jax.random.fold_in(key_list[8], 71), 0)
    return dict(query=query, keys=keys, values=values, memory_keys=memory_keys, memory_values=memory_values, routes=routes, documents=documents, cotangent=cotangent)


NEGATIVE = -1e+30

def reference(query, keys, values, memory_keys, memory_values, routes, documents, cotangent):
    scaling = 1.0 / math.sqrt(HDIM)
    window = REACH * TOK_DEV
    slot_rows = N_CTX * CAP * BLK
    owner = jnp.repeat(routes[:, 0], BLK)

    def one_head(head):
        start = head * HDIM
        head_query = lax.dynamic_slice_in_dim(query, start, HDIM, 1)
        head_keys = lax.dynamic_slice_in_dim(keys, start, HDIM, 1)
        head_values = lax.dynamic_slice_in_dim(values, start, HDIM, 1)
        head_memory_keys = lax.dynamic_slice_in_dim(memory_keys, start, HDIM, 1)
        head_memory_values = lax.dynamic_slice_in_dim(memory_values, start, HDIM, 1)
        head_upstream = lax.dynamic_slice_in_dim(cotangent, start, HDIM, 1)

        def block_step(carry, block):
            key_total, value_total = carry
            first = (block * TOK_DEV).astype(jnp.int32)
            lowest = jnp.clip((block - REACH + 1) * TOK_DEV, 0, TOKENS - window).astype(jnp.int32)
            query_rows = lax.dynamic_slice_in_dim(head_query, first, TOK_DEV, 0)
            near_keys = lax.dynamic_slice_in_dim(head_keys, lowest, window, 0)
            near_values = lax.dynamic_slice_in_dim(head_values, lowest, window, 0)
            upstream = lax.dynamic_slice_in_dim(head_upstream, first, TOK_DEV, 0)
            query_docs = lax.dynamic_slice_in_dim(documents, first, TOK_DEV, 0)
            key_docs = lax.dynamic_slice_in_dim(documents, lowest, window, 0)
            query_pos = first + jnp.arange(TOK_DEV, dtype=jnp.int32)
            key_pos = lowest + jnp.arange(window, dtype=jnp.int32)
            current_mask = (key_pos[None, :] <= query_pos[:, None]) & (key_docs[None, :] == query_docs[:, None])
            picked = jnp.argsort((owner != block).astype(jnp.int32), stable=True)[:slot_rows].astype(jnp.int32)
            block_memory_keys = jnp.take(head_memory_keys, picked, axis=0)
            block_memory_values = jnp.take(head_memory_values, picked, axis=0)
            live = jnp.take(owner, picked) == block
            memory_mask = jnp.broadcast_to(live[None, :], (TOK_DEV, slot_rows))
            current_scores = jnp.dot(query_rows, near_keys.T, preferred_element_type=jnp.float32) * scaling
            memory_scores = jnp.dot(query_rows, block_memory_keys.T, preferred_element_type=jnp.float32) * scaling
            top = jnp.maximum(lax.optimization_barrier(jnp.max(jnp.where(current_mask, current_scores, NEGATIVE), axis=1)), lax.optimization_barrier(jnp.max(jnp.where(memory_mask, memory_scores, NEGATIVE), axis=1)))
            current_weight = jnp.where(current_mask, jnp.exp(current_scores - top[:, None]), 0.0)
            memory_weight = jnp.where(memory_mask, jnp.exp(memory_scores - top[:, None]), 0.0)
            total = lax.optimization_barrier(jnp.sum(current_weight, axis=1)) + lax.optimization_barrier(jnp.sum(memory_weight, axis=1))
            mixed = jnp.dot(current_weight.astype(jnp.bfloat16), near_values, preferred_element_type=jnp.float32)
            mixed = mixed + jnp.dot(memory_weight.astype(jnp.bfloat16), block_memory_values, preferred_element_type=jnp.float32)
            output = mixed / total[:, None]
            log_total = top + jnp.log(total)
            delta = lax.optimization_barrier(jnp.sum(upstream.astype(jnp.float32) * output, axis=1))
            current_prob = jnp.where(current_mask, jnp.exp(current_scores - log_total[:, None]), 0.0)
            memory_prob = jnp.where(memory_mask, jnp.exp(memory_scores - log_total[:, None]), 0.0)
            current_press = jnp.dot(upstream, near_values.T, preferred_element_type=jnp.float32)
            memory_press = jnp.dot(upstream, block_memory_values.T, preferred_element_type=jnp.float32)
            current_sgrad = (current_prob * (current_press - delta[:, None])).astype(jnp.bfloat16)
            memory_sgrad = (memory_prob * (memory_press - delta[:, None])).astype(jnp.bfloat16)
            query_part = jnp.dot(current_sgrad, near_keys, preferred_element_type=jnp.float32)
            query_part = (query_part + jnp.dot(memory_sgrad, block_memory_keys, preferred_element_type=jnp.float32)) * scaling
            key_part = jnp.dot(current_sgrad.T, query_rows, preferred_element_type=jnp.float32) * scaling
            value_part = jnp.dot(current_prob.astype(jnp.bfloat16).T, upstream, preferred_element_type=jnp.float32)
            key_total = lax.dynamic_update_slice_in_dim(key_total, lax.dynamic_slice_in_dim(key_total, lowest, window, 0) + key_part, lowest, 0)
            value_total = lax.dynamic_update_slice_in_dim(value_total, lax.dynamic_slice_in_dim(value_total, lowest, window, 0) + value_part, lowest, 0)
            return ((key_total, value_total), (output.astype(jnp.bfloat16), query_part))
        zeros = jnp.zeros((TOKENS, HDIM), jnp.float32)
        (key_total, value_total), (outputs, query_parts) = lax.scan(block_step, (zeros, zeros), jnp.arange(N_CTX, dtype=jnp.int32))
        return (outputs.reshape(TOKENS, HDIM), query_parts.reshape(TOKENS, HDIM), key_total, value_total)
    outputs, query_all, key_all, value_all = lax.map(one_head, jnp.arange(HEADS, dtype=jnp.int32))
    squares = jnp.sum(query_all * query_all) + jnp.sum(key_all * key_all) + jnp.sum(value_all * value_all)
    spread = jnp.sqrt(squares / (3.0 * TOKENS * HEADS * HDIM) + 1e-06)

    def arrange(array):
        return jnp.transpose(array, (1, 0, 2)).reshape(TOKENS, HEADS * HDIM)
    return (arrange(outputs), arrange(query_all / spread).astype(jnp.bfloat16), arrange(key_all / spread).astype(jnp.bfloat16), arrange(value_all / spread).astype(jnp.bfloat16))
```

```python
import math

import jax
import jax.numpy as jnp
from jax import lax
from jax.experimental import pallas as pl
from jax.experimental.pallas import tpu as pltpu
from jax.sharding import PartitionSpec as P

HDIM = 128
BLK = 8
CAP = 2
NEGATIVE = -1e30
LOG2E = 1.4426950408889634
F32 = jnp.float32
BF16 = jnp.bfloat16


def dot_nt(a, b):
    return lax.dot_general(a, b, (((1,), (1,)), ((), ())), preferred_element_type=F32)


def dot_nn(a, b):
    return lax.dot_general(a, b, (((1,), (0,)), ((), ())), preferred_element_type=F32)


def shifted(value, steps):
    count = lax.axis_size("ctx")
    pairs = [(i, i + steps) for i in range(count) if 0 <= i + steps < count]
    return lax.ppermute(value, "ctx", pairs)


def swapped(value):
    count = lax.axis_size("ctx")
    return lax.ppermute(value, "ctx", [(i, i ^ 1) for i in range(count)])


def cost(flops, size, exps=0):
    return pl.CostEstimate(flops=int(flops), bytes_accessed=int(size), transcendentals=int(exps))


def pack_memory(my_routes, memory_keys, memory_values, count):
    blocks = memory_keys.shape[0] // BLK
    width = memory_keys.shape[1]
    half = width // 2

    def body(routes_ref, mk_ref, mv_ref, out_ref, used):
        out_ref[...] = jnp.zeros_like(out_ref)
        for owner in range(count):
            used[owner] = 0

        def place(block, carry):
            owner = routes_ref[block]
            slot = used[owner]
            used[owner] = slot + 1
            partner = owner + 1 - 2 * (owner % 2)
            near = pl.multiple_of((owner % 2) * half, half)
            far = pl.multiple_of(half - (owner % 2) * half, half)
            out_ref[owner, 0, slot, :, :half] = mk_ref[block, :, pl.ds(near, half)]
            out_ref[owner, 0, slot, :, half:] = mv_ref[block, :, pl.ds(near, half)]
            out_ref[partner, 1, slot, :, :half] = mk_ref[block, :, pl.ds(far, half)]
            out_ref[partner, 1, slot, :, half:] = mv_ref[block, :, pl.ds(far, half)]
            return carry

        lax.fori_loop(0, blocks, place, 0)

    return pl.pallas_call(
        body,
        out_shape=jax.ShapeDtypeStruct((count, 2, CAP, BLK, width), BF16),
        in_specs=[
            pl.BlockSpec(memory_space=pltpu.SMEM),
            pl.BlockSpec(memory_space=pltpu.VMEM),
            pl.BlockSpec(memory_space=pltpu.VMEM),
        ],
        out_specs=pl.BlockSpec(memory_space=pltpu.VMEM),
        scratch_shapes=[pltpu.SMEM((count,), jnp.int32)],
        cost_estimate=cost(0, 4 * memory_keys.size * 2),
        name="pack_memory",
    )(
        my_routes,
        memory_keys.reshape(blocks, BLK, width),
        memory_values.reshape(blocks, BLK, width),
    )


def visible_bias(key_doc, key_pos, query_doc, query_pos):
    return jnp.where((key_doc == query_doc) & (key_pos <= query_pos), 0.0, NEGATIVE)


class Plan:
    def __init__(self, rows, half, memory_rows):
        self.rows, self.half, self.memory_rows = rows, half, memory_rows
        self.heads = half // HDIM
        self.group = 2 if self.heads % 2 == 0 else 1
        self.steps = self.heads // self.group
        self.cols = self.group * HDIM
        self.scale = 1.0 / math.sqrt(HDIM)

    def first(self):
        return pl.BlockSpec((self.rows, self.cols), lambda i: (0, i))

    def second(self):
        return pl.BlockSpec((self.rows, self.cols), lambda i: (0, self.steps + i))

    def memory(self, part):
        slots = self.memory_rows // (CAP * BLK)
        return pl.BlockSpec(
            (slots, 2, CAP * BLK, self.cols), lambda i: (0, 0, 0, part * self.steps + i)
        )

    def whole(self, shape):
        return pl.BlockSpec(shape, lambda i: (0,) * len(shape))

    def stacked(self):
        return pl.BlockSpec((2, self.rows, self.cols), lambda i: (0, 0, i))


def joined(refs, lanes):
    return jnp.concatenate([ref[:, lanes] for ref in refs], axis=0)


def scores_of(plan, query, key_refs, memory_ref, bias, memory_bias_ref, lanes, rows):
    scaling = plan.scale * LOG2E
    keys = joined(key_refs, lanes)
    current = dot_nt(query, keys) * scaling + bias
    parts, memory_keys = [], []
    for part in range(2):
        mem = memory_ref[:, part, :, lanes].reshape(plan.memory_rows, HDIM)
        score = dot_nt(query[part * rows : (part + 1) * rows], mem)
        parts.append(score * scaling + memory_bias_ref[part : part + 1, :])
        memory_keys.append(mem)
    return keys, memory_keys, current, jnp.concatenate(parts, axis=0)


def forward(plan, own_qd, far_qd, kv, memory, key_row, query_col, memory_bias):
    rows = plan.rows

    def body(
        qo, qf, do_o, do_f, k0, k1, k2, k3, v0, v1, v2, v3, mk, mv, krow, qcol, mbias,
        att_own, att_far, stat_col, stat_row,
    ):
        bias = visible_bias(krow[0:1, :], krow[1:2, :], qcol[:, 0:1], qcol[:, 1:2])
        lane = lax.broadcasted_iota(jnp.int32, (2 * rows, HDIM), 1)
        stats = jnp.zeros((2 * rows, HDIM), F32)
        for g in range(plan.group):
            lanes = slice(g * HDIM, (g + 1) * HDIM)
            query = joined((qo, qf), lanes)
            _, _, current, mem = scores_of(
                plan, query, (k0, k1, k2, k3), mk, bias, mbias, lanes, rows
            )
            top = jnp.maximum(
                jnp.max(current, axis=1, keepdims=True), jnp.max(mem, axis=1, keepdims=True)
            )
            weight = jnp.exp2(current - top)
            mem_weight = jnp.exp2(mem - top)
            total = jnp.sum(weight, axis=1, keepdims=True) + jnp.sum(
                mem_weight, axis=1, keepdims=True
            )
            values = joined((v0, v1, v2, v3), lanes)
            mixed = dot_nn(weight.astype(BF16), values)
            mem16 = mem_weight.astype(BF16)
            mixed_mem = [
                dot_nn(
                    mem16[part * rows : (part + 1) * rows],
                    mv[:, part, :, lanes].reshape(plan.memory_rows, HDIM),
                )
                for part in range(2)
            ]
            output = (mixed + jnp.concatenate(mixed_mem, axis=0)) / total
            upstream = joined((do_o, do_f), lanes).astype(F32)
            delta = jnp.sum(upstream * output, axis=1, keepdims=True)
            level = top + jnp.log2(total)
            stats = jnp.where(lane == g, level, stats)
            stats = jnp.where(lane == plan.group + g, delta, stats)
            att_own[:, lanes] = output[:rows].astype(BF16)
            att_far[:, lanes] = output[rows:].astype(BF16)
        stat_col[0] = stats
        stat_row[0] = stats.T[0:8, :]

    flops = 2 * 2 * (2 * rows) * (4 * rows + plan.memory_rows) * plan.half
    return pl.pallas_call(
        body,
        grid=(plan.steps,),
        out_shape=(
            jax.ShapeDtypeStruct((rows, plan.half), BF16),
            jax.ShapeDtypeStruct((rows, plan.half), BF16),
            jax.ShapeDtypeStruct((plan.steps, 2 * rows, HDIM), F32),
            jax.ShapeDtypeStruct((plan.steps, 8, 2 * rows), F32),
        ),
        in_specs=[plan.first()] * 2
        + [plan.second()] * 2
        + [plan.first()] * 4
        + [plan.second()] * 4
        + [plan.memory(0), plan.memory(1)]
        + [plan.whole(key_row.shape), plan.whole(query_col.shape), plan.whole(memory_bias.shape)],
        out_specs=(
            plan.first(),
            plan.first(),
            pl.BlockSpec((1, 2 * rows, HDIM), lambda i: (i, 0, 0)),
            pl.BlockSpec((1, 8, 2 * rows), lambda i: (i, 0, 0)),
        ),
        cost_estimate=cost(flops, 12 * rows * plan.half * 2, 2 * rows * 5 * rows * plan.heads),
        name="attend",
    )(own_qd, far_qd, own_qd, far_qd, *kv, *kv, memory, memory, key_row, query_col, memory_bias)


def query_gradient(plan, own_qd, far_qd, kv, memory, key_row, query_col, memory_bias, stats, att):
    rows = plan.rows

    def body(
        qo, qf, do_o, do_f, k0, k1, k2, k3, v0, v1, v2, v3, mk, mv, krow, qcol, mbias,
        stat_col, att_far, dq_own, send, squares,
    ):
        bias = visible_bias(krow[0:1, :], krow[1:2, :], qcol[:, 0:1], qcol[:, 1:2])
        acc = jnp.zeros((8, HDIM), F32)
        for g in range(plan.group):
            lanes = slice(g * HDIM, (g + 1) * HDIM)
            query = joined((qo, qf), lanes)
            upstream = joined((do_o, do_f), lanes)
            level = stat_col[0, :, g : g + 1]
            delta = stat_col[0, :, plan.group + g : plan.group + g + 1]
            keys, mem_keys, current, mem = scores_of(
                plan, query, (k0, k1, k2, k3), mk, bias, mbias, lanes, rows
            )
            values = joined((v0, v1, v2, v3), lanes)
            press = dot_nt(upstream, values) - delta
            grad = (jnp.exp2(current - level) * press).astype(BF16)
            result = dot_nn(grad, keys)
            extra = []
            for part in range(2):
                span = slice(part * rows, (part + 1) * rows)
                mem_values = mv[:, part, :, lanes].reshape(plan.memory_rows, HDIM)
                mem_press = dot_nt(upstream[span], mem_values) - delta[span]
                mem_grad = (jnp.exp2(mem[span] - level[span]) * mem_press).astype(BF16)
                extra.append(dot_nn(mem_grad, mem_keys[part]))
            result = (result + jnp.concatenate(extra, axis=0)) * plan.scale
            dq_own[:, lanes] = result[:rows]
            send[0, :, lanes] = result[rows:].astype(BF16)
            acc = acc + jnp.sum((result * result).reshape(-1, 8, HDIM), axis=0)
        send[1] = att_far[...]

        @pl.when(pl.program_id(0) == 0)
        def _():
            squares[...] = jnp.zeros_like(squares)

        squares[...] += acc

    flops = 3 * 2 * (2 * rows) * (4 * rows + plan.memory_rows) * plan.half
    return pl.pallas_call(
        body,
        grid=(plan.steps,),
        out_shape=(
            jax.ShapeDtypeStruct((rows, plan.half), F32),
            jax.ShapeDtypeStruct((2, rows, plan.half), BF16),
            jax.ShapeDtypeStruct((8, HDIM), F32),
        ),
        in_specs=[plan.first()] * 2
        + [plan.second()] * 2
        + [plan.first()] * 4
        + [plan.second()] * 4
        + [plan.memory(0), plan.memory(1)]
        + [plan.whole(key_row.shape), plan.whole(query_col.shape), plan.whole(memory_bias.shape)]
        + [pl.BlockSpec((1, 2 * rows, HDIM), lambda i: (i, 0, 0)), plan.first()],
        out_specs=(plan.first(), plan.stacked(), plan.whole((8, HDIM))),
        cost_estimate=cost(flops, 14 * rows * plan.half * 2, 2 * rows * 5 * rows * plan.heads),
        name="query_gradient",
    )(
        own_qd, far_qd, own_qd, far_qd, *kv, *kv, memory, memory, key_row, query_col, memory_bias,
        stats, att,
    )


def key_terms(plan, key, value, query, upstream, bias, level, delta):
    score = dot_nt(key, query) * (plan.scale * LOG2E) + bias
    prob = jnp.exp2(score - level)
    grad = (prob * (dot_nt(value, upstream) - delta)).astype(BF16)
    return dot_nn(grad, query) * plan.scale, dot_nn(prob.astype(BF16), upstream)


def key_gradient_near(plan, own_qd, far_qd, own_kv, far_kv, query_row, key_col, stats):
    rows = plan.rows

    def body(qo, qf, do_o, do_f, k0, k1, v0, v1, qrow, kcol, stat, dk, dv):
        bias = visible_bias(kcol[:, 0:1], kcol[:, 1:2], qrow[0:1, :], qrow[1:2, :])
        for g in range(plan.group):
            lanes = slice(g * HDIM, (g + 1) * HDIM)
            key_part, value_part = key_terms(
                plan,
                joined((k0, k1), lanes),
                joined((v0, v1), lanes),
                joined((qo, qf), lanes),
                joined((do_o, do_f), lanes),
                bias,
                stat[0, g : g + 1, :],
                stat[0, plan.group + g : plan.group + g + 1, :],
            )
            dk[:, lanes] = key_part
            dv[:, lanes] = value_part

    both = pl.BlockSpec((2 * rows, plan.cols), lambda i: (0, i))
    return pl.pallas_call(
        body,
        grid=(plan.steps,),
        out_shape=(jax.ShapeDtypeStruct((2 * rows, plan.half), F32),) * 2,
        in_specs=[plan.first()] * 2
        + [plan.second()] * 2
        + [plan.first()] * 2
        + [plan.second()] * 2
        + [plan.whole(query_row.shape), plan.whole(key_col.shape)]
        + [pl.BlockSpec((1, 8, 2 * rows), lambda i: (i, 0, 0))],
        out_specs=(both, both),
        cost_estimate=cost(
            4 * 2 * (2 * rows) ** 2 * plan.half, 16 * rows * plan.half * 2, 4 * rows * rows * plan.heads
        ),
        name="key_gradient_near",
    )(own_qd, far_qd, own_qd, far_qd, own_kv, far_kv, own_kv, far_kv, query_row, key_col, stats)


def key_gradient_next(
    plan, own_qd, far_qd, own_kv, far_kv, query_row, key_col, stats, near_dk, near_dv, dq_squares, devices
):
    rows = plan.rows

    def body(
        qo, qf, do_o, do_f, k0, k1, v0, v1, qrow, kcol, stat, dk_in, dv_in, dq_sq,
        dk_own, dv_own, send, share, squares,
    ):
        bias = visible_bias(kcol[:, 0:1], kcol[:, 1:2], qrow[0:1, :], qrow[1:2, :])
        acc = jnp.zeros((8, HDIM), F32)
        for g in range(plan.group):
            lanes = slice(g * HDIM, (g + 1) * HDIM)
            key_part, value_part = key_terms(
                plan,
                joined((k0, k1), lanes),
                joined((v0, v1), lanes),
                joined((qo, qf), lanes),
                joined((do_o, do_f), lanes),
                bias,
                stat[0, g : g + 1, :],
                stat[0, plan.group + g : plan.group + g + 1, :],
            )
            key_part = key_part + dk_in[:, lanes]
            value_part = value_part + dv_in[:, lanes]
            dk_own[:, lanes] = key_part[:rows]
            dv_own[:, lanes] = value_part[:rows]
            send[0, :, lanes] = key_part[rows:].astype(BF16)
            send[1, :, lanes] = value_part[rows:].astype(BF16)
            both = key_part * key_part + value_part * value_part
            acc = acc + jnp.sum(both.reshape(-1, 8, HDIM), axis=0)

        @pl.when(pl.program_id(0) == 0)
        def _():
            squares[...] = dq_sq[...]

        squares[...] += acc

        @pl.when(pl.program_id(0) == plan.steps - 1)
        def _():
            row = jnp.sum(squares[...], axis=0, keepdims=True)
            share[...] = jnp.broadcast_to(row, share.shape)

    both = pl.BlockSpec((2 * rows, plan.cols), lambda i: (0, i))
    return pl.pallas_call(
        body,
        grid=(plan.steps,),
        out_shape=(
            jax.ShapeDtypeStruct((rows, plan.half), F32),
            jax.ShapeDtypeStruct((rows, plan.half), F32),
            jax.ShapeDtypeStruct((2, rows, plan.half), BF16),
            jax.ShapeDtypeStruct((devices, HDIM), F32),
        ),
        in_specs=[plan.first()] * 2
        + [plan.second()] * 2
        + [plan.first()] * 2
        + [plan.second()] * 2
        + [plan.whole(query_row.shape), plan.whole(key_col.shape)]
        + [pl.BlockSpec((1, 8, 2 * rows), lambda i: (i, 0, 0)), both, both]
        + [plan.whole((8, HDIM))],
        out_specs=(plan.first(), plan.first(), plan.stacked(), plan.whole((devices, HDIM))),
        scratch_shapes=[pltpu.VMEM((8, HDIM), F32)],
        cost_estimate=cost(
            4 * 2 * (2 * rows) ** 2 * plan.half, 24 * rows * plan.half * 2, 4 * rows * rows * plan.heads
        ),
        name="key_gradient_next",
    )(
        own_qd, far_qd, own_qd, far_qd, own_kv, far_kv, own_kv, far_kv, query_row, key_col, stats,
        near_dk, near_dv, dq_squares,
    )


def scaled(plan, side, shares, entries, dq_own, dq_far, dk_own, dv_own, kv_far):
    rows, half = plan.rows, plan.half

    def body(side_ref, share, dq, dq_other, dk, dv, other, dq_out, dk_out, dv_out):
        squares = jnp.sum(jnp.sum(share[...], axis=0, keepdims=True), axis=1, keepdims=True)
        inverse = 1.0 / jnp.sqrt(squares / entries + 1e-06)
        near = pl.multiple_of(side_ref[0] * half, half)
        away = pl.multiple_of(half - side_ref[0] * half, half)
        for out, mine, theirs in (
            (dq_out, dq[...], dq_other[0]),
            (dk_out, dk[...], other[0]),
            (dv_out, dv[...], other[1]),
        ):
            out[:, pl.ds(near, half)] = (mine * inverse).astype(BF16)
            out[:, pl.ds(away, half)] = (theirs.astype(F32) * inverse).astype(BF16)

    vmem = pl.BlockSpec(memory_space=pltpu.VMEM)
    return pl.pallas_call(
        body,
        out_shape=(jax.ShapeDtypeStruct((rows, 2 * half), BF16),) * 3,
        in_specs=[pl.BlockSpec(memory_space=pltpu.SMEM)] + [vmem] * 6,
        out_specs=(vmem,) * 3,
        cost_estimate=cost(6 * rows * half, 20 * rows * half),
        name="scaled",
    )(side, shares, dq_own, dq_far, dk_own, dv_own, kv_far)


def on_device(query, keys, values, memory_keys, memory_values, routes, documents, cotangent):
    rows, width = query.shape
    half = width // 2
    count = lax.axis_size("ctx")
    devices = count * lax.axis_size("head")
    position = lax.axis_index("ctx").astype(jnp.int32)
    side = position % 2
    partner = position + 1 - 2 * side
    per_device = memory_keys.shape[0] // BLK
    memory_rows = count * CAP * BLK
    plan = Plan(rows, half, memory_rows)

    def halves(left, right, which):
        start = which * half
        return jnp.concatenate(
            [
                lax.dynamic_slice(left, (0, start), (rows, half)),
                lax.dynamic_slice(right, (0, start), (rows, half)),
            ],
            axis=1,
        )

    own_kv = halves(keys, values, side)
    own_qd = halves(query, cotangent, side)
    far_kv = swapped(halves(keys, values, 1 - side))
    far_qd = swapped(halves(query, cotangent, 1 - side))
    route_table = routes[:, 0].reshape(count, per_device)
    my_routes = lax.dynamic_slice_in_dim(routes[:, 0], position * per_device, per_device)
    packed = pack_memory(my_routes, memory_keys, memory_values, count)
    arrived = lax.all_to_all(
        packed.reshape(count, 2 * CAP * BLK, width), "ctx", split_axis=0, concat_axis=0, tiled=True
    ).reshape(count, 2, CAP * BLK, width)
    prev_own_kv = shifted(own_kv, 2)
    prev_far_kv = shifted(far_kv, 2)
    next_own_qd = shifted(own_qd, -2)
    next_far_qd = shifted(far_qd, -2)

    def labels(block):
        docs = lax.dynamic_slice_in_dim(documents, block * rows, rows)
        docs = jnp.where((block >= 0) & (block < count), docs, -1)
        return jnp.stack([docs, block * rows + jnp.arange(rows, dtype=jnp.int32)])

    near_row = jnp.concatenate([labels(position), labels(partner)], axis=1)
    prev_row = jnp.concatenate([labels(position - 2), labels(partner - 2)], axis=1)
    next_row = jnp.concatenate([labels(position + 2), labels(partner + 2)], axis=1)
    key_row = jnp.concatenate([near_row, prev_row], axis=1)
    near_col = near_row.T
    readers = jnp.stack([position, partner])
    arrivals = jnp.sum((route_table[None] == readers[:, None, None]).astype(jnp.int32), axis=2)
    live = jnp.arange(CAP, dtype=jnp.int32)[None, None, :] < arrivals[:, :, None]
    memory_bias = jnp.broadcast_to(
        jnp.where(live, 0.0, NEGATIVE)[..., None], (2, count, CAP, BLK)
    ).reshape(2, memory_rows)

    kv = (own_kv, far_kv, prev_own_kv, prev_far_kv)
    att_own, att_far, stat_col, stat_row = forward(
        plan, own_qd, far_qd, kv, arrived, key_row, near_col, memory_bias
    )
    next_stats = shifted(stat_row, -2)
    dq_own, first_send, dq_squares = query_gradient(
        plan, own_qd, far_qd, kv, arrived, key_row, near_col, memory_bias, stat_col, att_far
    )
    first_back = swapped(first_send)
    near_dk, near_dv = key_gradient_near(
        plan, own_qd, far_qd, own_kv, far_kv, near_row, near_col, stat_row
    )
    dk_own, dv_own, second_send, share = key_gradient_next(
        plan, next_own_qd, next_far_qd, own_kv, far_kv, next_row, near_col, next_stats,
        near_dk, near_dv, dq_squares, devices,
    )
    second_back = swapped(second_send)
    shares = lax.all_to_all(share, ("ctx", "head"), split_axis=0, concat_axis=0, tiled=True)
    entries = 3.0 * count * rows * width * lax.axis_size("head")
    query_grad, key_grad, value_grad = scaled(
        plan, side[None], shares, entries, dq_own, first_back, dk_own, dv_own, second_back
    )
    att_back = first_back[1]
    attended = jnp.where(
        side == 0,
        jnp.concatenate([att_own, att_back], axis=1),
        jnp.concatenate([att_back, att_own], axis=1),
    )
    return attended, query_grad, key_grad, value_grad


def solution(mesh):
    spread = P("ctx", "head")
    return jax.shard_map(
        on_device,
        mesh=mesh,
        in_specs=(spread,) * 5 + (P(), P(), spread),
        out_specs=(spread,) * 4,
        check_vma=False,
    )
```

```python
import math

import jax
import jax.numpy as jnp
from jax import lax
from jax.experimental import pallas as pl
from jax.experimental.pallas import tpu as pltpu
from jax.sharding import PartitionSpec as P

HDIM = 128
BLK = 8
CAP = 2
NEGATIVE = -1e30
LOG2E = 1.4426950408889634
F32 = jnp.float32
BF16 = jnp.bfloat16
VMEM_BYTES = 20 * 2**20


def dot_nt(a, b):
    return lax.dot_general(a, b, (((1,), (1,)), ((), ())), preferred_element_type=F32)


def dot_nn(a, b):
    return lax.dot_general(a, b, (((1,), (0,)), ((), ())), preferred_element_type=F32)


def shifted(value, steps):
    count = lax.axis_size("ctx")
    pairs = [(i, i + steps) for i in range(count) if 0 <= i + steps < count]
    return lax.ppermute(value, "ctx", pairs)


def swapped(value):
    count = lax.axis_size("ctx")
    return lax.ppermute(value, "ctx", [(i, i ^ 1) for i in range(count)])


def cost(flops, size, exps=0):
    return pl.CostEstimate(flops=int(flops), bytes_accessed=int(size), transcendentals=int(exps))


def staged(position, routes, query, keys, values, cotangent, memory_keys, memory_values, count):
    rows, width = keys.shape
    half = width // 2
    blocks = memory_keys.shape[0] // BLK

    def body(
        where, routes_ref, q, k, v, do, mk, mv, own_kv, far_kv, own_qd, far_qd, packed, used, cut_sem, block_sem
    ):
        side = where[0] % 2
        kept = pl.ds(pl.multiple_of(side * half, half), half)
        sent = pl.ds(pl.multiple_of(half - side * half, half), half)
        left, right = pl.ds(0, half), pl.ds(half, half)
        cuts = [
            (k, sent, far_kv, left),
            (v, sent, far_kv, right),
            (k, kept, own_kv, left),
            (v, kept, own_kv, right),
            (q, kept, own_qd, left),
            (do, kept, own_qd, right),
            (q, sent, far_qd, left),
            (do, sent, far_qd, right),
        ]
        copies = [
            pltpu.make_async_copy(src.at[:, cols], dst.at[:, part], cut_sem.at[n])
            for n, (src, cols, dst, part) in enumerate(cuts)
        ]
        for copy in copies:
            copy.start()
        packed[...] = jnp.zeros_like(packed)
        for owner in range(count):
            used[owner] = 0

        def place(block, carry):
            owner = routes_ref[where[0] * blocks + block]
            slot = used[owner]
            used[owner] = slot + 1
            odd = owner % 2
            partner = owner + 1 - 2 * odd
            near = pl.ds(pl.multiple_of(odd * half, half), half)
            away = pl.ds(pl.multiple_of(half - odd * half, half), half)
            for n, (src, cols, target, who, part) in enumerate(
                (
                    (mk, near, owner, 0, left),
                    (mv, near, owner, 0, right),
                    (mk, away, partner, 1, left),
                    (mv, away, partner, 1, right),
                )
            ):
                pltpu.make_async_copy(
                    src.at[block, :, cols], packed.at[target, who, slot, :, part], block_sem.at[block, n]
                ).start()
            return carry

        lax.fori_loop(0, blocks, place, 0)

        def settle(block, carry):
            for n in range(4):
                pltpu.make_async_copy(
                    mk.at[block, :, left], packed.at[0, 0, 0, :, left], block_sem.at[block, n]
                ).wait()
            return carry

        lax.fori_loop(0, blocks, settle, 0)
        for copy in copies:
            copy.wait()

    smem = pl.BlockSpec(memory_space=pltpu.SMEM)
    hbm = pl.BlockSpec(memory_space=pltpu.HBM)
    flat = jax.ShapeDtypeStruct((rows, width), BF16)
    return pl.pallas_call(
        body,
        out_shape=(flat,) * 4 + (jax.ShapeDtypeStruct((count, 2, CAP, BLK, width), BF16),),
        in_specs=[smem] * 2 + [hbm] * 6,
        out_specs=(pl.BlockSpec(memory_space=pltpu.VMEM),) * 5,
        scratch_shapes=[
            pltpu.SMEM((count,), jnp.int32),
            pltpu.SemaphoreType.DMA((8,)),
            pltpu.SemaphoreType.DMA((blocks, 4)),
        ],
        cost_estimate=cost(0, 2 * (4 * rows + 2 * blocks * BLK) * width * 2),
        compiler_params=pltpu.CompilerParams(vmem_limit_bytes=60 * 2**20),
        name="staged",
    )(
        position[None],
        routes.reshape(-1),
        query,
        keys,
        values,
        cotangent,
        memory_keys.reshape(blocks, BLK, width),
        memory_values.reshape(blocks, BLK, width),
    )


def visible_bias(key_doc, key_pos, query_doc, query_pos):
    return jnp.where((key_doc == query_doc) & (key_pos <= query_pos), 0.0, NEGATIVE)


class Plan:
    def __init__(self, rows, half, memory_rows):
        self.rows, self.half, self.memory_rows = rows, half, memory_rows
        self.heads = half // HDIM
        self.group = math.gcd(self.heads, 4)
        self.steps = self.heads // self.group
        self.cols = self.group * HDIM
        self.scale = 1.0 / math.sqrt(HDIM)

    def first(self):
        return pl.BlockSpec((self.rows, self.cols), lambda i: (0, i))

    def second(self):
        return pl.BlockSpec((self.rows, self.cols), lambda i: (0, self.steps + i))

    def memory(self, part):
        slots = self.memory_rows // (CAP * BLK)
        return pl.BlockSpec(
            (slots, 2, CAP * BLK, self.cols), lambda i: (0, 0, 0, part * self.steps + i)
        )

    def whole(self, shape):
        return pl.BlockSpec(shape, lambda i: (0,) * len(shape))

    def stacked(self):
        return pl.BlockSpec((2, self.rows, self.cols), lambda i: (0, 0, i))


def joined(refs, lanes):
    return jnp.concatenate([ref[:, lanes] for ref in refs], axis=0)


def scores_of(plan, query, key_refs, memory_ref, bias, memory_bias_ref, lanes, rows):
    scaling = plan.scale * LOG2E
    keys = joined(key_refs, lanes)
    current = dot_nt(query, keys) * scaling + bias
    parts, memory_keys = [], []
    for part in range(2):
        mem = memory_ref[:, part, :, lanes].reshape(plan.memory_rows, HDIM)
        score = dot_nt(query[part * rows : (part + 1) * rows], mem)
        parts.append(score * scaling + memory_bias_ref[part : part + 1, :])
        memory_keys.append(mem)
    return keys, memory_keys, current, jnp.concatenate(parts, axis=0)


def forward(plan, own_qd, far_qd, kv, memory, key_row, query_col, memory_bias):
    rows = plan.rows

    def body(
        qo, qf, do_o, do_f, k0, k1, k2, k3, v0, v1, v2, v3, mk, mv, krow, qcol, mbias,
        att_own, att_far, stat_col, stat_row,
    ):
        bias = visible_bias(krow[0:1, :], krow[1:2, :], qcol[:, 0:1], qcol[:, 1:2])
        lane = lax.broadcasted_iota(jnp.int32, (2 * rows, HDIM), 1)
        stats = jnp.zeros((2 * rows, HDIM), F32)
        for g in range(plan.group):
            lanes = slice(g * HDIM, (g + 1) * HDIM)
            query = joined((qo, qf), lanes)
            _, _, current, mem = scores_of(
                plan, query, (k0, k1, k2, k3), mk, bias, mbias, lanes, rows
            )
            top = jnp.maximum(
                jnp.max(current, axis=1, keepdims=True), jnp.max(mem, axis=1, keepdims=True)
            )
            weight = jnp.exp2(current - top)
            mem_weight = jnp.exp2(mem - top)
            total = jnp.sum(weight, axis=1, keepdims=True) + jnp.sum(
                mem_weight, axis=1, keepdims=True
            )
            values = joined((v0, v1, v2, v3), lanes)
            mixed = dot_nn(weight.astype(BF16), values)
            mem16 = mem_weight.astype(BF16)
            mixed_mem = [
                dot_nn(
                    mem16[part * rows : (part + 1) * rows],
                    mv[:, part, :, lanes].reshape(plan.memory_rows, HDIM),
                )
                for part in range(2)
            ]
            output = (mixed + jnp.concatenate(mixed_mem, axis=0)) / total
            upstream = joined((do_o, do_f), lanes).astype(F32)
            delta = jnp.sum(upstream * output, axis=1, keepdims=True)
            level = top + jnp.log2(total)
            stats = jnp.where(lane == g, level, stats)
            stats = jnp.where(lane == plan.group + g, delta, stats)
            att_own[:, lanes] = output[:rows].astype(BF16)
            att_far[:, lanes] = output[rows:].astype(BF16)
        stat_col[0] = stats
        stat_row[0] = stats.T[0:8, :]

    flops = 2 * 2 * (2 * rows) * (4 * rows + plan.memory_rows) * plan.half
    return pl.pallas_call(
        body,
        grid=(plan.steps,),
        out_shape=(
            jax.ShapeDtypeStruct((rows, plan.half), BF16),
            jax.ShapeDtypeStruct((rows, plan.half), BF16),
            jax.ShapeDtypeStruct((plan.steps, 2 * rows, HDIM), F32),
            jax.ShapeDtypeStruct((plan.steps, 8, 2 * rows), F32),
        ),
        in_specs=[plan.first()] * 2
        + [plan.second()] * 2
        + [plan.first()] * 4
        + [plan.second()] * 4
        + [plan.memory(0), plan.memory(1)]
        + [plan.whole(key_row.shape), plan.whole(query_col.shape), plan.whole(memory_bias.shape)],
        out_specs=(
            plan.first(),
            plan.first(),
            pl.BlockSpec((1, 2 * rows, HDIM), lambda i: (i, 0, 0)),
            pl.BlockSpec((1, 8, 2 * rows), lambda i: (i, 0, 0)),
        ),
        cost_estimate=cost(flops, 12 * rows * plan.half * 2, 2 * rows * 5 * rows * plan.heads),
        compiler_params=pltpu.CompilerParams(vmem_limit_bytes=VMEM_BYTES),
        name="attend",
    )(own_qd, far_qd, own_qd, far_qd, *kv, *kv, memory, memory, key_row, query_col, memory_bias)


def dot_tn(a, b):
    return lax.dot_general(a, b, (((0,), (0,)), ((), ())), preferred_element_type=F32)


def own_gradients(plan, own_qd, far_qd, kv, memory, key_row, query_col, memory_bias, stats):
    rows = plan.rows

    def body(
        qo, qf, do_o, do_f, k0, k1, k2, k3, v0, v1, v2, v3, mk, mv, krow, qcol, mbias,
        stat_col, dq_own, dq_far, squares, dk, dv,
    ):
        bias = visible_bias(krow[0:1, :], krow[1:2, :], qcol[:, 0:1], qcol[:, 1:2])
        acc = jnp.zeros((8, HDIM), F32)
        for g in range(plan.group):
            lanes = slice(g * HDIM, (g + 1) * HDIM)
            query = joined((qo, qf), lanes)
            upstream = joined((do_o, do_f), lanes)
            level = stat_col[0, :, g : g + 1]
            delta = stat_col[0, :, plan.group + g : plan.group + g + 1]
            keys, mem_keys, current, mem = scores_of(
                plan, query, (k0, k1, k2, k3), mk, bias, mbias, lanes, rows
            )
            values = joined((v0, v1, v2, v3), lanes)
            press = dot_nt(upstream, values) - delta
            prob = jnp.exp2(current - level)
            grad = (prob * press).astype(BF16)
            result = dot_nn(grad, keys)
            extra = []
            for part in range(2):
                span = slice(part * rows, (part + 1) * rows)
                mem_values = mv[:, part, :, lanes].reshape(plan.memory_rows, HDIM)
                mem_press = dot_nt(upstream[span], mem_values) - delta[span]
                mem_grad = (jnp.exp2(mem[span] - level[span]) * mem_press).astype(BF16)
                extra.append(dot_nn(mem_grad, mem_keys[part]))
            result = (result + jnp.concatenate(extra, axis=0)) * plan.scale
            dq_own[:, lanes] = result[:rows]
            dq_far[:, lanes] = result[rows:].astype(BF16)
            acc = acc + jnp.sum((result * result).reshape(-1, 8, HDIM), axis=0)
            dk[:, lanes] = dot_tn(grad[:, : 2 * rows], query) * plan.scale
            dv[:, lanes] = dot_tn(prob[:, : 2 * rows].astype(BF16), upstream)

        @pl.when(pl.program_id(0) == 0)
        def _():
            squares[...] = jnp.zeros_like(squares)

        squares[...] += acc

    both = pl.BlockSpec((2 * rows, plan.cols), lambda i: (0, i))
    flops = (3 * (4 * rows + plan.memory_rows) + 4 * rows) * 2 * (2 * rows) * plan.half
    return pl.pallas_call(
        body,
        grid=(plan.steps,),
        out_shape=(
            jax.ShapeDtypeStruct((rows, plan.half), F32),
            jax.ShapeDtypeStruct((rows, plan.half), BF16),
            jax.ShapeDtypeStruct((8, HDIM), F32),
            jax.ShapeDtypeStruct((2 * rows, plan.half), F32),
            jax.ShapeDtypeStruct((2 * rows, plan.half), F32),
        ),
        in_specs=[plan.first()] * 2
        + [plan.second()] * 2
        + [plan.first()] * 4
        + [plan.second()] * 4
        + [plan.memory(0), plan.memory(1)]
        + [plan.whole(key_row.shape), plan.whole(query_col.shape), plan.whole(memory_bias.shape)]
        + [pl.BlockSpec((1, 2 * rows, HDIM), lambda i: (i, 0, 0))],
        out_specs=(plan.first(), plan.first(), plan.whole((8, HDIM)), both, both),
        cost_estimate=cost(flops, 22 * rows * plan.half * 2, 2 * rows * 5 * rows * plan.heads),
        compiler_params=pltpu.CompilerParams(vmem_limit_bytes=VMEM_BYTES),
        name="own_gradients",
    )(
        own_qd, far_qd, own_qd, far_qd, *kv, *kv, memory, memory, key_row, query_col, memory_bias,
        stats,
    )


def key_terms(plan, key, value, query, upstream, bias, level, delta):
    score = dot_nt(key, query) * (plan.scale * LOG2E) + bias
    prob = jnp.exp2(score - level)
    grad = (prob * (dot_nt(value, upstream) - delta)).astype(BF16)
    return dot_nn(grad, query) * plan.scale, dot_nn(prob.astype(BF16), upstream)


def key_gradient_next(
    plan, own_qd, far_qd, own_kv, far_kv, query_row, key_col, stats, near_dk, near_dv, dq_squares, devices
):
    rows = plan.rows

    def body(
        qo, qf, do_o, do_f, k0, k1, v0, v1, qrow, kcol, stat, dk_in, dv_in, dq_sq,
        dk_own, dv_own, send, share, squares,
    ):
        bias = visible_bias(kcol[:, 0:1], kcol[:, 1:2], qrow[0:1, :], qrow[1:2, :])
        acc = jnp.zeros((8, HDIM), F32)
        for g in range(plan.group):
            lanes = slice(g * HDIM, (g + 1) * HDIM)
            key_part, value_part = key_terms(
                plan,
                joined((k0, k1), lanes),
                joined((v0, v1), lanes),
                joined((qo, qf), lanes),
                joined((do_o, do_f), lanes),
                bias,
                stat[0, g : g + 1, :],
                stat[0, plan.group + g : plan.group + g + 1, :],
            )
            key_part = key_part + dk_in[:, lanes]
            value_part = value_part + dv_in[:, lanes]
            dk_own[:, lanes] = key_part[:rows]
            dv_own[:, lanes] = value_part[:rows]
            send[0, :, lanes] = key_part[rows:].astype(BF16)
            send[1, :, lanes] = value_part[rows:].astype(BF16)
            both = key_part * key_part + value_part * value_part
            acc = acc + jnp.sum(both.reshape(-1, 8, HDIM), axis=0)

        @pl.when(pl.program_id(0) == 0)
        def _():
            squares[...] = dq_sq[...]

        squares[...] += acc

        @pl.when(pl.program_id(0) == plan.steps - 1)
        def _():
            row = jnp.sum(squares[...], axis=0, keepdims=True)
            share[...] = jnp.broadcast_to(row, share.shape)

    both = pl.BlockSpec((2 * rows, plan.cols), lambda i: (0, i))
    return pl.pallas_call(
        body,
        grid=(plan.steps,),
        out_shape=(
            jax.ShapeDtypeStruct((rows, plan.half), F32),
            jax.ShapeDtypeStruct((rows, plan.half), F32),
            jax.ShapeDtypeStruct((2, rows, plan.half), BF16),
            jax.ShapeDtypeStruct((devices, HDIM), F32),
        ),
        in_specs=[plan.first()] * 2
        + [plan.second()] * 2
        + [plan.first()] * 2
        + [plan.second()] * 2
        + [plan.whole(query_row.shape), plan.whole(key_col.shape)]
        + [pl.BlockSpec((1, 8, 2 * rows), lambda i: (i, 0, 0)), both, both]
        + [plan.whole((8, HDIM))],
        out_specs=(plan.first(), plan.first(), plan.stacked(), plan.whole((devices, HDIM))),
        scratch_shapes=[pltpu.VMEM((8, HDIM), F32)],
        cost_estimate=cost(
            4 * 2 * (2 * rows) ** 2 * plan.half, 24 * rows * plan.half * 2, 4 * rows * rows * plan.heads
        ),
        compiler_params=pltpu.CompilerParams(vmem_limit_bytes=VMEM_BYTES),
        name="key_gradient_next",
    )(
        own_qd, far_qd, own_qd, far_qd, own_kv, far_kv, own_kv, far_kv, query_row, key_col, stats,
        near_dk, near_dv, dq_squares,
    )


def scaled(plan, side, shares, entries, dq_own, dq_far, dk_own, dv_own, kv_far):
    rows, half = plan.rows, plan.half

    def body(side_ref, share, dq, dq_other, dk, dv, other, dq_out, dk_out, dv_out):
        squares = jnp.sum(jnp.sum(share[...], axis=0, keepdims=True), axis=1, keepdims=True)
        inverse = 1.0 / jnp.sqrt(squares / entries + 1e-06)
        near = pl.multiple_of(side_ref[0] * half, half)
        away = pl.multiple_of(half - side_ref[0] * half, half)
        for out, mine, theirs in (
            (dq_out, dq[...], dq_other[...]),
            (dk_out, dk[...], other[0]),
            (dv_out, dv[...], other[1]),
        ):
            out[:, pl.ds(near, half)] = (mine * inverse).astype(BF16)
            out[:, pl.ds(away, half)] = (theirs.astype(F32) * inverse).astype(BF16)

    vmem = pl.BlockSpec(memory_space=pltpu.VMEM)
    return pl.pallas_call(
        body,
        out_shape=(jax.ShapeDtypeStruct((rows, 2 * half), BF16),) * 3,
        in_specs=[pl.BlockSpec(memory_space=pltpu.SMEM)] + [vmem] * 6,
        out_specs=(vmem,) * 3,
        cost_estimate=cost(6 * rows * half, 20 * rows * half),
        compiler_params=pltpu.CompilerParams(vmem_limit_bytes=VMEM_BYTES),
        name="scaled",
    )(side, shares, dq_own, dq_far, dk_own, dv_own, kv_far)


def on_device(query, keys, values, memory_keys, memory_values, routes, documents, cotangent):
    rows, width = query.shape
    half = width // 2
    count = lax.axis_size("ctx")
    devices = count * lax.axis_size("head")
    position = lax.axis_index("ctx").astype(jnp.int32)
    side = position % 2
    partner = position + 1 - 2 * side
    per_device = memory_keys.shape[0] // BLK
    memory_rows = count * CAP * BLK
    plan = Plan(rows, half, memory_rows)

    own_kv, sent_kv, own_qd, sent_qd, packed = staged(
        position, routes, query, keys, values, cotangent, memory_keys, memory_values, count
    )
    far_kv = swapped(sent_kv)
    prev_own_kv = shifted(own_kv, 2)
    next_own_qd = shifted(own_qd, -2)
    far_kv, sent_qd = lax.optimization_barrier((far_kv, sent_qd))
    prev_far_kv = shifted(far_kv, 2)
    far_qd = swapped(sent_qd)
    route_table = routes[:, 0].reshape(count, per_device)
    arrived = lax.all_to_all(
        packed.reshape(count, 2 * CAP * BLK, width), "ctx", split_axis=0, concat_axis=0, tiled=True
    ).reshape(count, 2, CAP * BLK, width)
    next_far_qd = shifted(far_qd, -2)

    def labels(block):
        docs = lax.dynamic_slice_in_dim(documents, block * rows, rows)
        docs = jnp.where((block >= 0) & (block < count), docs, -1)
        return jnp.stack([docs, block * rows + jnp.arange(rows, dtype=jnp.int32)])

    near_row = jnp.concatenate([labels(position), labels(partner)], axis=1)
    prev_row = jnp.concatenate([labels(position - 2), labels(partner - 2)], axis=1)
    next_row = jnp.concatenate([labels(position + 2), labels(partner + 2)], axis=1)
    key_row = jnp.concatenate([near_row, prev_row], axis=1)
    near_col = near_row.T
    readers = jnp.stack([position, partner])
    arrivals = jnp.sum((route_table[None] == readers[:, None, None]).astype(jnp.int32), axis=2)
    live = jnp.arange(CAP, dtype=jnp.int32)[None, None, :] < arrivals[:, :, None]
    memory_bias = jnp.broadcast_to(
        jnp.where(live, 0.0, NEGATIVE)[..., None], (2, count, CAP, BLK)
    ).reshape(2, memory_rows)

    kv = (own_kv, far_kv, prev_own_kv, prev_far_kv)
    att_own, att_far, stat_col, stat_row = forward(
        plan, own_qd, far_qd, kv, arrived, key_row, near_col, memory_bias
    )
    next_stats = shifted(stat_row, -2)
    att_back = swapped(att_far)
    dq_own, dq_far, dq_squares, near_dk, near_dv = own_gradients(
        plan, own_qd, far_qd, kv, arrived, key_row, near_col, memory_bias, stat_col
    )
    next_stats, dq_far, att_back = lax.optimization_barrier((next_stats, dq_far, att_back))
    dq_back = swapped(dq_far)
    dk_own, dv_own, second_send, share = key_gradient_next(
        plan, next_own_qd, next_far_qd, own_kv, far_kv, next_row, near_col, next_stats,
        near_dk, near_dv, dq_squares, devices,
    )
    second_send, dq_back = lax.optimization_barrier((second_send, dq_back))
    second_back = swapped(second_send)
    shares = lax.all_to_all(share, ("ctx", "head"), split_axis=0, concat_axis=0, tiled=True)
    entries = 3.0 * count * rows * width * lax.axis_size("head")
    query_grad, key_grad, value_grad = scaled(
        plan, side[None], shares, entries, dq_own, dq_back, dk_own, dv_own, second_back
    )
    attended = jnp.where(
        side == 0,
        jnp.concatenate([att_own, att_back], axis=1),
        jnp.concatenate([att_back, att_own], axis=1),
    )
    return attended, query_grad, key_grad, value_grad


def solution(mesh):
    spread = P("ctx", "head")
    return jax.shard_map(
        on_device,
        mesh=mesh,
        in_specs=(spread,) * 5 + (P(), P(), spread),
        out_specs=(spread,) * 4,
        check_vma=False,
    )
```

```python
import math

import jax
import jax.numpy as jnp
from jax import lax
from jax.experimental import pallas as pl
from jax.experimental.pallas import tpu as pltpu
from jax.sharding import PartitionSpec as P

HDIM = 128
BLK = 8
CAP = 2
NEGATIVE = -1e30
LOG2E = 1.4426950408889634
F32 = jnp.float32
BF16 = jnp.bfloat16
VMEM_BYTES = 20 * 2**20


def dot_nt(a, b):
    return lax.dot_general(a, b, (((1,), (1,)), ((), ())), preferred_element_type=F32)


def dot_nn(a, b):
    return lax.dot_general(a, b, (((1,), (0,)), ((), ())), preferred_element_type=F32)


def shifted(value, steps):
    count = lax.axis_size("ctx")
    pairs = [(i, i + steps) for i in range(count) if 0 <= i + steps < count]
    return lax.ppermute(value, "ctx", pairs)


def swapped(value):
    count = lax.axis_size("ctx")
    return lax.ppermute(value, "ctx", [(i, i ^ 1) for i in range(count)])


def cost(flops, size, exps=0):
    return pl.CostEstimate(flops=int(flops), bytes_accessed=int(size), transcendentals=int(exps))


def halves(position, left, right):
    rows, width = left.shape
    half = width // 2

    def body(where, one, two, kept, sent, sems):
        side = where[0] % 2
        near = pl.ds(pl.multiple_of(side * half, half), half)
        away = pl.ds(pl.multiple_of(half - side * half, half), half)
        cuts = [(away, sent), (near, kept)]
        copies = []
        for n, (cols, out) in enumerate(cuts):
            for m, src in enumerate((one, two)):
                dst = out.at[:, pl.ds(m * half, half)]
                copies.append(pltpu.make_async_copy(src.at[:, cols], dst, sems.at[n, m]))
        for copy in copies:
            copy.start()
        for copy in copies:
            copy.wait()

    hbm = pl.BlockSpec(memory_space=pltpu.HBM)
    return pl.pallas_call(
        body,
        out_shape=(jax.ShapeDtypeStruct((rows, width), BF16),) * 2,
        in_specs=[pl.BlockSpec(memory_space=pltpu.SMEM), hbm, hbm],
        out_specs=(pl.BlockSpec(memory_space=pltpu.VMEM),) * 2,
        scratch_shapes=[pltpu.SemaphoreType.DMA((2, 2))],
        cost_estimate=cost(0, 4 * rows * width * 2),
        compiler_params=pltpu.CompilerParams(vmem_limit_bytes=60 * 2**20),
        name="halves",
    )(position[None], left, right)


def pack_memory(position, routes, memory_keys, memory_values, count):
    blocks = memory_keys.shape[0] // BLK
    width = memory_keys.shape[1]
    half = width // 2

    def body(where, routes_ref, mk, mv, packed, used, sems):
        left, right = pl.ds(0, half), pl.ds(half, half)
        packed[...] = jnp.zeros_like(packed)
        for owner in range(count):
            used[owner] = 0

        def place(block, carry):
            owner = routes_ref[where[0] * blocks + block]
            slot = used[owner]
            used[owner] = slot + 1
            odd = owner % 2
            partner = owner + 1 - 2 * odd
            near = pl.ds(pl.multiple_of(odd * half, half), half)
            away = pl.ds(pl.multiple_of(half - odd * half, half), half)
            for n, (src, cols, target, who, part) in enumerate(
                (
                    (mk, near, owner, 0, left),
                    (mv, near, owner, 0, right),
                    (mk, away, partner, 1, left),
                    (mv, away, partner, 1, right),
                )
            ):
                pltpu.make_async_copy(
                    src.at[block, :, cols], packed.at[target, who, slot, :, part], sems.at[block, n]
                ).start()
            return carry

        lax.fori_loop(0, blocks, place, 0)

        def settle(block, carry):
            for n in range(4):
                pltpu.make_async_copy(
                    mk.at[block, :, left], packed.at[0, 0, 0, :, left], sems.at[block, n]
                ).wait()
            return carry

        lax.fori_loop(0, blocks, settle, 0)

    smem = pl.BlockSpec(memory_space=pltpu.SMEM)
    hbm = pl.BlockSpec(memory_space=pltpu.HBM)
    return pl.pallas_call(
        body,
        out_shape=jax.ShapeDtypeStruct((count, 2, CAP, BLK, width), BF16),
        in_specs=[smem, smem, hbm, hbm],
        out_specs=pl.BlockSpec(memory_space=pltpu.VMEM),
        scratch_shapes=[pltpu.SMEM((count,), jnp.int32), pltpu.SemaphoreType.DMA((blocks, 4))],
        cost_estimate=cost(0, 4 * memory_keys.size * 2),
        compiler_params=pltpu.CompilerParams(vmem_limit_bytes=60 * 2**20),
        name="pack_memory",
    )(
        position[None],
        routes.reshape(-1),
        memory_keys.reshape(blocks, BLK, width),
        memory_values.reshape(blocks, BLK, width),
    )


def visible_bias(key_doc, key_pos, query_doc, query_pos):
    return jnp.where((key_doc == query_doc) & (key_pos <= query_pos), 0.0, NEGATIVE)


class Plan:
    def __init__(self, rows, half, memory_rows):
        self.rows, self.half, self.memory_rows = rows, half, memory_rows
        self.heads = half // HDIM
        self.group = math.gcd(self.heads, 4)
        self.steps = self.heads // self.group
        self.cols = self.group * HDIM
        self.scale = 1.0 / math.sqrt(HDIM)

    def first(self):
        return pl.BlockSpec((self.rows, self.cols), lambda i: (0, i))

    def second(self):
        return pl.BlockSpec((self.rows, self.cols), lambda i: (0, self.steps + i))

    def memory(self, part):
        slots = self.memory_rows // (CAP * BLK)
        return pl.BlockSpec(
            (slots, 2, CAP * BLK, self.cols), lambda i: (0, 0, 0, part * self.steps + i)
        )

    def pair(self):
        return pl.BlockSpec((2 * self.rows, self.cols), lambda i: (0, i))

    def whole(self, shape):
        return pl.BlockSpec(shape, lambda i: (0,) * len(shape))

    def stacked(self):
        return pl.BlockSpec((2, self.rows, self.cols), lambda i: (0, 0, i))


def joined(refs, lanes):
    return jnp.concatenate([ref[:, lanes] for ref in refs], axis=0)


def scores_of(plan, query, key_refs, memory_ref, bias, memory_bias_ref, lanes, rows):
    scaling = plan.scale * LOG2E
    keys = joined(key_refs, lanes)
    current = dot_nt(query, keys) * scaling + bias
    parts, memory_keys = [], []
    for part in range(2):
        mem = memory_ref[:, part, :, lanes].reshape(plan.memory_rows, HDIM)
        score = dot_nt(query[part * rows : (part + 1) * rows], mem)
        parts.append(score * scaling + memory_bias_ref[part : part + 1, :])
        memory_keys.append(mem)
    return keys, memory_keys, current, jnp.concatenate(parts, axis=0)


def widened(column, like):
    return jnp.concatenate([column] * (like.shape[1] // column.shape[1]), axis=1)


def attend_near(plan, own_qd, far_qd, kv, memory, key_row, query_col, memory_bias):
    rows = plan.rows

    def body(qo, qf, k0, k1, v0, v1, mk, mv, krow, qcol, mbias, mixed_out, top_out, total_out):
        bias = visible_bias(krow[0:1, :], krow[1:2, :], qcol[:, 0:1], qcol[:, 1:2])
        for g in range(plan.group):
            lanes = slice(g * HDIM, (g + 1) * HDIM)
            query = joined((qo, qf), lanes)
            _, _, current, mem = scores_of(plan, query, (k0, k1), mk, bias, mbias, lanes, rows)
            top = jnp.maximum(
                jnp.max(current, axis=1, keepdims=True), jnp.max(mem, axis=1, keepdims=True)
            )
            weight = jnp.exp2(current - top)
            mem_weight = jnp.exp2(mem - top)
            total = jnp.sum(weight, axis=1, keepdims=True) + jnp.sum(
                mem_weight, axis=1, keepdims=True
            )
            mixed = dot_nn(weight.astype(BF16), joined((v0, v1), lanes))
            mem16 = mem_weight.astype(BF16)
            mixed_mem = [
                dot_nn(
                    mem16[part * rows : (part + 1) * rows],
                    mv[:, part, :, lanes].reshape(plan.memory_rows, HDIM),
                )
                for part in range(2)
            ]
            mixed_out[:, lanes] = mixed + jnp.concatenate(mixed_mem, axis=0)
            top_out[:, lanes] = jnp.broadcast_to(top, (2 * rows, HDIM))
            total_out[:, lanes] = jnp.broadcast_to(total, (2 * rows, HDIM))

    flops = 2 * 2 * (2 * rows) * (2 * rows + plan.memory_rows) * plan.half
    return pl.pallas_call(
        body,
        grid=(plan.steps,),
        out_shape=(jax.ShapeDtypeStruct((2 * rows, plan.half), F32),) * 3,
        in_specs=[plan.first()] * 4
        + [plan.second()] * 2
        + [plan.memory(0), plan.memory(1)]
        + [plan.whole(key_row.shape), plan.whole(query_col.shape), plan.whole(memory_bias.shape)],
        out_specs=(plan.pair(),) * 3,
        cost_estimate=cost(flops, 12 * rows * plan.half * 2, 2 * rows * 3 * rows * plan.heads),
        compiler_params=pltpu.CompilerParams(vmem_limit_bytes=VMEM_BYTES),
        name="attend_near",
    )(own_qd, far_qd, *kv, *kv, memory, memory, key_row, query_col, memory_bias)


def attend_prev(plan, own_qd, far_qd, kv, key_row, query_col, near):
    rows = plan.rows

    def body(
        qo, qf, do_o, do_f, k0, k1, v0, v1, krow, qcol, mixed_in, top_in, total_in,
        att_own, att_far, level_out, delta_out, stat_row,
    ):
        bias = visible_bias(krow[0:1, :], krow[1:2, :], qcol[:, 0:1], qcol[:, 1:2])
        lane = lax.broadcasted_iota(jnp.int32, (2 * rows, HDIM), 1)
        stats = jnp.zeros((2 * rows, HDIM), F32)
        scaling = plan.scale * LOG2E
        for g in range(plan.group):
            lanes = slice(g * HDIM, (g + 1) * HDIM)
            query = joined((qo, qf), lanes)
            score = dot_nt(query, joined((k0, k1), lanes)) * scaling + bias
            near_top = top_in[:, lanes]
            top = jnp.maximum(
                jnp.broadcast_to(jnp.max(score, axis=1, keepdims=True), near_top.shape), near_top
            )
            weight = jnp.exp2(score - widened(top, score))
            shrink = jnp.exp2(near_top - top)
            total = jnp.sum(weight, axis=1, keepdims=True) + total_in[:, lanes] * shrink
            mixed = dot_nn(weight.astype(BF16), joined((v0, v1), lanes))
            output = (mixed + mixed_in[:, lanes] * shrink) / total
            upstream = joined((do_o, do_f), lanes).astype(F32)
            delta = jnp.sum(upstream * output, axis=1, keepdims=True)
            level = top + jnp.log2(total)
            stats = jnp.where(lane == g, level, stats)
            stats = jnp.where(lane == plan.group + g, delta, stats)
            level_out[:, lanes] = level
            delta_out[:, lanes] = jnp.broadcast_to(delta, level.shape)
            att_own[:, lanes] = output[:rows].astype(BF16)
            att_far[:, lanes] = output[rows:].astype(BF16)
        stat_row[0] = stats.T[0:8, :]

    flops = 2 * 2 * (2 * rows) * (2 * rows) * plan.half
    return pl.pallas_call(
        body,
        grid=(plan.steps,),
        out_shape=(
            jax.ShapeDtypeStruct((rows, plan.half), BF16),
            jax.ShapeDtypeStruct((rows, plan.half), BF16),
            jax.ShapeDtypeStruct((2 * rows, plan.half), F32),
            jax.ShapeDtypeStruct((2 * rows, plan.half), F32),
            jax.ShapeDtypeStruct((plan.steps, 8, 2 * rows), F32),
        ),
        in_specs=[plan.first()] * 2
        + [plan.second()] * 2
        + [plan.first()] * 2
        + [plan.second()] * 2
        + [plan.whole(key_row.shape), plan.whole(query_col.shape)]
        + [plan.pair()] * 3,
        out_specs=(
            plan.first(),
            plan.first(),
            plan.pair(),
            plan.pair(),
            pl.BlockSpec((1, 8, 2 * rows), lambda i: (i, 0, 0)),
        ),
        cost_estimate=cost(flops, 16 * rows * plan.half * 2, 4 * rows * rows * plan.heads),
        compiler_params=pltpu.CompilerParams(vmem_limit_bytes=VMEM_BYTES),
        name="attend_prev",
    )(
        own_qd, far_qd, own_qd, far_qd, *kv, *kv, key_row, query_col, *near
    )


def dot_tn(a, b):
    return lax.dot_general(a, b, (((0,), (0,)), ((), ())), preferred_element_type=F32)


def own_gradients(plan, own_qd, far_qd, kv, memory, key_row, query_col, memory_bias, level, delta):
    rows = plan.rows

    def body(
        qo, qf, do_o, do_f, k0, k1, k2, k3, v0, v1, v2, v3, mk, mv, krow, qcol, mbias,
        level_in, delta_in, dq_own, dq_far, squares, dk, dv,
    ):
        bias = visible_bias(krow[0:1, :], krow[1:2, :], qcol[:, 0:1], qcol[:, 1:2])
        acc = jnp.zeros((8, HDIM), F32)
        for g in range(plan.group):
            lanes = slice(g * HDIM, (g + 1) * HDIM)
            query = joined((qo, qf), lanes)
            upstream = joined((do_o, do_f), lanes)
            level = level_in[:, lanes]
            delta = delta_in[:, lanes]
            keys, mem_keys, current, mem = scores_of(
                plan, query, (k0, k1, k2, k3), mk, bias, mbias, lanes, rows
            )
            values = joined((v0, v1, v2, v3), lanes)
            press = dot_nt(upstream, values) - widened(delta, current)
            prob = jnp.exp2(current - widened(level, current))
            grad = (prob * press).astype(BF16)
            result = dot_nn(grad, keys)
            extra = []
            for part in range(2):
                span = slice(part * rows, (part + 1) * rows)
                mem_values = mv[:, part, :, lanes].reshape(plan.memory_rows, HDIM)
                mem_press = dot_nt(upstream[span], mem_values) - widened(delta[span], mem)
                mem_grad = (jnp.exp2(mem[span] - widened(level[span], mem)) * mem_press).astype(BF16)
                extra.append(dot_nn(mem_grad, mem_keys[part]))
            result = (result + jnp.concatenate(extra, axis=0)) * plan.scale
            dq_own[:, lanes] = result[:rows]
            dq_far[:, lanes] = result[rows:].astype(BF16)
            acc = acc + jnp.sum((result * result).reshape(-1, 8, HDIM), axis=0)
            dk[:, lanes] = dot_tn(grad[:, : 2 * rows], query) * plan.scale
            dv[:, lanes] = dot_tn(prob[:, : 2 * rows].astype(BF16), upstream)

        @pl.when(pl.program_id(0) == 0)
        def _():
            squares[...] = jnp.zeros_like(squares)

        squares[...] += acc

    both = pl.BlockSpec((2 * rows, plan.cols), lambda i: (0, i))
    flops = (3 * (4 * rows + plan.memory_rows) + 4 * rows) * 2 * (2 * rows) * plan.half
    return pl.pallas_call(
        body,
        grid=(plan.steps,),
        out_shape=(
            jax.ShapeDtypeStruct((rows, plan.half), F32),
            jax.ShapeDtypeStruct((rows, plan.half), BF16),
            jax.ShapeDtypeStruct((8, HDIM), F32),
            jax.ShapeDtypeStruct((2 * rows, plan.half), F32),
            jax.ShapeDtypeStruct((2 * rows, plan.half), F32),
        ),
        in_specs=[plan.first()] * 2
        + [plan.second()] * 2
        + [plan.first()] * 4
        + [plan.second()] * 4
        + [plan.memory(0), plan.memory(1)]
        + [plan.whole(key_row.shape), plan.whole(query_col.shape), plan.whole(memory_bias.shape)]
        + [plan.pair()] * 2,
        out_specs=(plan.first(), plan.first(), plan.whole((8, HDIM)), both, both),
        cost_estimate=cost(flops, 22 * rows * plan.half * 2, 2 * rows * 5 * rows * plan.heads),
        compiler_params=pltpu.CompilerParams(vmem_limit_bytes=VMEM_BYTES),
        name="own_gradients",
    )(
        own_qd, far_qd, own_qd, far_qd, *kv, *kv, memory, memory, key_row, query_col, memory_bias,
        level, delta,
    )


def key_terms(plan, key, value, query, upstream, bias, level, delta):
    score = dot_nt(key, query) * (plan.scale * LOG2E) + bias
    prob = jnp.exp2(score - level)
    grad = (prob * (dot_nt(value, upstream) - delta)).astype(BF16)
    return dot_nn(grad, query) * plan.scale, dot_nn(prob.astype(BF16), upstream)


def key_gradient_next(
    plan, own_qd, far_qd, own_kv, far_kv, query_row, key_col, stats, near_dk, near_dv, dq_squares, devices
):
    rows = plan.rows

    def body(
        qo, qf, do_o, do_f, k0, k1, v0, v1, qrow, kcol, stat, dk_in, dv_in, dq_sq,
        dk_own, dv_own, send, share, squares,
    ):
        bias = visible_bias(kcol[:, 0:1], kcol[:, 1:2], qrow[0:1, :], qrow[1:2, :])
        acc = jnp.zeros((8, HDIM), F32)
        for g in range(plan.group):
            lanes = slice(g * HDIM, (g + 1) * HDIM)
            key_part, value_part = key_terms(
                plan,
                joined((k0, k1), lanes),
                joined((v0, v1), lanes),
                joined((qo, qf), lanes),
                joined((do_o, do_f), lanes),
                bias,
                stat[0, g : g + 1, :],
                stat[0, plan.group + g : plan.group + g + 1, :],
            )
            key_part = key_part + dk_in[:, lanes]
            value_part = value_part + dv_in[:, lanes]
            dk_own[:, lanes] = key_part[:rows]
            dv_own[:, lanes] = value_part[:rows]
            send[0, :, lanes] = key_part[rows:].astype(BF16)
            send[1, :, lanes] = value_part[rows:].astype(BF16)
            both = key_part * key_part + value_part * value_part
            acc = acc + jnp.sum(both.reshape(-1, 8, HDIM), axis=0)

        @pl.when(pl.program_id(0) == 0)
        def _():
            squares[...] = dq_sq[...]

        squares[...] += acc

        @pl.when(pl.program_id(0) == plan.steps - 1)
        def _():
            row = jnp.sum(squares[...], axis=0, keepdims=True)
            share[...] = jnp.broadcast_to(row, share.shape)

    both = pl.BlockSpec((2 * rows, plan.cols), lambda i: (0, i))
    return pl.pallas_call(
        body,
        grid=(plan.steps,),
        out_shape=(
            jax.ShapeDtypeStruct((rows, plan.half), F32),
            jax.ShapeDtypeStruct((rows, plan.half), F32),
            jax.ShapeDtypeStruct((2, rows, plan.half), BF16),
            jax.ShapeDtypeStruct((devices, HDIM), F32),
        ),
        in_specs=[plan.first()] * 2
        + [plan.second()] * 2
        + [plan.first()] * 2
        + [plan.second()] * 2
        + [plan.whole(query_row.shape), plan.whole(key_col.shape)]
        + [pl.BlockSpec((1, 8, 2 * rows), lambda i: (i, 0, 0)), both, both]
        + [plan.whole((8, HDIM))],
        out_specs=(plan.first(), plan.first(), plan.stacked(), plan.whole((devices, HDIM))),
        scratch_shapes=[pltpu.VMEM((8, HDIM), F32)],
        cost_estimate=cost(
            4 * 2 * (2 * rows) ** 2 * plan.half, 24 * rows * plan.half * 2, 4 * rows * rows * plan.heads
        ),
        compiler_params=pltpu.CompilerParams(vmem_limit_bytes=VMEM_BYTES),
        name="key_gradient_next",
    )(
        own_qd, far_qd, own_qd, far_qd, own_kv, far_kv, own_kv, far_kv, query_row, key_col, stats,
        near_dk, near_dv, dq_squares,
    )


def scaled(plan, side, shares, entries, dq_own, dq_far, dk_own, dv_own, kv_far):
    rows, half = plan.rows, plan.half

    def body(side_ref, share, dq, dq_other, dk, dv, other, dq_out, dk_out, dv_out):
        squares = jnp.sum(jnp.sum(share[...], axis=0, keepdims=True), axis=1, keepdims=True)
        inverse = 1.0 / jnp.sqrt(squares / entries + 1e-06)
        near = pl.multiple_of(side_ref[0] * half, half)
        away = pl.multiple_of(half - side_ref[0] * half, half)
        for out, mine, theirs in (
            (dq_out, dq[...], dq_other[...]),
            (dk_out, dk[...], other[0]),
            (dv_out, dv[...], other[1]),
        ):
            out[:, pl.ds(near, half)] = (mine * inverse).astype(BF16)
            out[:, pl.ds(away, half)] = (theirs.astype(F32) * inverse).astype(BF16)

    vmem = pl.BlockSpec(memory_space=pltpu.VMEM)
    return pl.pallas_call(
        body,
        out_shape=(jax.ShapeDtypeStruct((rows, 2 * half), BF16),) * 3,
        in_specs=[pl.BlockSpec(memory_space=pltpu.SMEM)] + [vmem] * 6,
        out_specs=(vmem,) * 3,
        cost_estimate=cost(6 * rows * half, 20 * rows * half),
        compiler_params=pltpu.CompilerParams(vmem_limit_bytes=VMEM_BYTES),
        name="scaled",
    )(side, shares, dq_own, dq_far, dk_own, dv_own, kv_far)


def on_device(query, keys, values, memory_keys, memory_values, routes, documents, cotangent):
    rows, width = query.shape
    half = width // 2
    count = lax.axis_size("ctx")
    devices = count * lax.axis_size("head")
    position = lax.axis_index("ctx").astype(jnp.int32)
    side = position % 2
    partner = position + 1 - 2 * side
    per_device = memory_keys.shape[0] // BLK
    memory_rows = count * CAP * BLK
    plan = Plan(rows, half, memory_rows)

    packed = pack_memory(position, routes, memory_keys, memory_values, count)
    own_kv, sent_kv = halves(position, keys, values)
    own_qd, sent_qd = halves(position, query, cotangent)
    far_kv = swapped(sent_kv)
    prev_own_kv = shifted(own_kv, 2)
    next_own_qd = shifted(own_qd, -2)
    far_kv, sent_qd = lax.optimization_barrier((far_kv, sent_qd))
    prev_far_kv = shifted(far_kv, 2)
    far_qd = swapped(sent_qd)
    route_table = routes[:, 0].reshape(count, per_device)
    arrived = lax.all_to_all(
        packed.reshape(count, 2 * CAP * BLK, width), "ctx", split_axis=0, concat_axis=0, tiled=True
    ).reshape(count, 2, CAP * BLK, width)
    next_far_qd = shifted(far_qd, -2)

    def labels(block):
        docs = lax.dynamic_slice_in_dim(documents, block * rows, rows)
        docs = jnp.where((block >= 0) & (block < count), docs, -1)
        return jnp.stack([docs, block * rows + jnp.arange(rows, dtype=jnp.int32)])

    near_row = jnp.concatenate([labels(position), labels(partner)], axis=1)
    prev_row = jnp.concatenate([labels(position - 2), labels(partner - 2)], axis=1)
    next_row = jnp.concatenate([labels(position + 2), labels(partner + 2)], axis=1)
    key_row = jnp.concatenate([near_row, prev_row], axis=1)
    near_col = near_row.T
    readers = jnp.stack([position, partner])
    arrivals = jnp.sum((route_table[None] == readers[:, None, None]).astype(jnp.int32), axis=2)
    live = jnp.arange(CAP, dtype=jnp.int32)[None, None, :] < arrivals[:, :, None]
    memory_bias = jnp.broadcast_to(
        jnp.where(live, 0.0, NEGATIVE)[..., None], (2, count, CAP, BLK)
    ).reshape(2, memory_rows)

    kv = (own_kv, far_kv, prev_own_kv, prev_far_kv)
    near = attend_near(plan, own_qd, far_qd, kv[:2], arrived, near_row, near_col, memory_bias)
    att_own, att_far, level, delta, stat_row = attend_prev(
        plan, own_qd, far_qd, kv[2:], prev_row, near_col, near
    )
    next_stats = shifted(stat_row, -2)
    att_back = swapped(att_far)
    dq_own, dq_far, dq_squares, near_dk, near_dv = own_gradients(
        plan, own_qd, far_qd, kv, arrived, key_row, near_col, memory_bias, level, delta
    )
    next_stats, dq_far, att_back = lax.optimization_barrier((next_stats, dq_far, att_back))
    dq_back = swapped(dq_far)
    dk_own, dv_own, second_send, share = key_gradient_next(
        plan, next_own_qd, next_far_qd, own_kv, far_kv, next_row, near_col, next_stats,
        near_dk, near_dv, dq_squares, devices,
    )
    second_send, dq_back = lax.optimization_barrier((second_send, dq_back))
    second_back = swapped(second_send)
    shares = lax.all_to_all(share, ("ctx", "head"), split_axis=0, concat_axis=0, tiled=True)
    entries = 3.0 * count * rows * width * lax.axis_size("head")
    query_grad, key_grad, value_grad = scaled(
        plan, side[None], shares, entries, dq_own, dq_back, dk_own, dv_own, second_back
    )
    attended = jnp.where(
        side == 0,
        jnp.concatenate([att_own, att_back], axis=1),
        jnp.concatenate([att_back, att_own], axis=1),
    )
    return attended, query_grad, key_grad, value_grad


def solution(mesh):
    spread = P("ctx", "head")
    return jax.shard_map(
        on_device,
        mesh=mesh,
        in_specs=(spread,) * 5 + (P(), P(), spread),
        out_specs=(spread,) * 4,
        check_vma=False,
    )
```

```python
import math

import jax
import jax.numpy as jnp
from jax import lax
from jax.experimental import pallas as pl
from jax.experimental.pallas import tpu as pltpu
from jax.sharding import PartitionSpec as P

HDIM = 128
BLK = 8
CAP = 2
NEGATIVE = -1e30
LOG2E = 1.4426950408889634
F32 = jnp.float32
BF16 = jnp.bfloat16
VMEM_BYTES = 20 * 2**20


def dot_nt(a, b):
    return lax.dot_general(a, b, (((1,), (1,)), ((), ())), preferred_element_type=F32)


def dot_nn(a, b):
    return lax.dot_general(a, b, (((1,), (0,)), ((), ())), preferred_element_type=F32)


def shifted(value, steps):
    count = lax.axis_size("ctx")
    pairs = [(i, i + steps) for i in range(count) if 0 <= i + steps < count]
    return lax.ppermute(value, "ctx", pairs)


def swapped(value):
    count = lax.axis_size("ctx")
    return lax.ppermute(value, "ctx", [(i, i ^ 1) for i in range(count)])


def cost(flops, size, exps=0):
    return pl.CostEstimate(flops=int(flops), bytes_accessed=int(size), transcendentals=int(exps))


def halves(position, left, right):
    rows, width = left.shape
    half = width // 2

    def body(where, one, two, kept, sent, sems):
        side = where[0] % 2
        near = pl.ds(pl.multiple_of(side * half, half), half)
        away = pl.ds(pl.multiple_of(half - side * half, half), half)
        cuts = [(away, sent), (near, kept)]
        copies = []
        for n, (cols, out) in enumerate(cuts):
            for m, src in enumerate((one, two)):
                dst = out.at[:, pl.ds(m * half, half)]
                copies.append(pltpu.make_async_copy(src.at[:, cols], dst, sems.at[n, m]))
        for copy in copies:
            copy.start()
        for copy in copies:
            copy.wait()

    hbm = pl.BlockSpec(memory_space=pltpu.HBM)
    return pl.pallas_call(
        body,
        out_shape=(jax.ShapeDtypeStruct((rows, width), BF16),) * 2,
        in_specs=[pl.BlockSpec(memory_space=pltpu.SMEM), hbm, hbm],
        out_specs=(pl.BlockSpec(memory_space=pltpu.VMEM),) * 2,
        scratch_shapes=[pltpu.SemaphoreType.DMA((2, 2))],
        cost_estimate=cost(0, 4 * rows * width * 2),
        compiler_params=pltpu.CompilerParams(vmem_limit_bytes=60 * 2**20),
        name="halves",
    )(position[None], left, right)


def pack_memory(position, routes, memory_keys, memory_values, count):
    blocks = memory_keys.shape[0] // BLK
    width = memory_keys.shape[1]
    half = width // 2

    def body(where, routes_ref, mk, mv, packed, keys, values, used, sems):
        copies = [
            pltpu.make_async_copy(mk, keys, sems.at[0]),
            pltpu.make_async_copy(mv, values, sems.at[1]),
        ]
        for copy in copies:
            copy.start()
        packed[...] = jnp.zeros_like(packed)
        for owner in range(count):
            used[owner] = 0
        for copy in copies:
            copy.wait()

        def place(block, carry):
            owner = routes_ref[where[0] * blocks + block]
            slot = used[owner]
            used[owner] = slot + 1
            odd = owner % 2
            partner = owner + 1 - 2 * odd
            near = pl.ds(pl.multiple_of(odd * half, half), half)
            away = pl.ds(pl.multiple_of(half - odd * half, half), half)
            packed[owner, 0, slot, :, :half] = keys[block, :, near]
            packed[owner, 0, slot, :, half:] = values[block, :, near]
            packed[partner, 1, slot, :, :half] = keys[block, :, away]
            packed[partner, 1, slot, :, half:] = values[block, :, away]
            return carry

        lax.fori_loop(0, blocks, place, 0)

    smem = pl.BlockSpec(memory_space=pltpu.SMEM)
    hbm = pl.BlockSpec(memory_space=pltpu.HBM)
    return pl.pallas_call(
        body,
        out_shape=jax.ShapeDtypeStruct((count, 2, CAP, BLK, width), BF16),
        in_specs=[smem, smem, hbm, hbm],
        out_specs=pl.BlockSpec(memory_space=pltpu.VMEM),
        scratch_shapes=[
            pltpu.VMEM((blocks, BLK, width), BF16),
            pltpu.VMEM((blocks, BLK, width), BF16),
            pltpu.SMEM((count,), jnp.int32),
            pltpu.SemaphoreType.DMA((2,)),
        ],
        cost_estimate=cost(0, 4 * memory_keys.size * 2),
        compiler_params=pltpu.CompilerParams(vmem_limit_bytes=60 * 2**20),
        name="pack_memory",
    )(
        position[None],
        routes.reshape(-1),
        memory_keys.reshape(blocks, BLK, width),
        memory_values.reshape(blocks, BLK, width),
    )


def visible_bias(key_doc, key_pos, query_doc, query_pos):
    return jnp.where((key_doc == query_doc) & (key_pos <= query_pos), 0.0, NEGATIVE)


class Plan:
    def __init__(self, rows, half, memory_rows):
        self.rows, self.half, self.memory_rows = rows, half, memory_rows
        self.heads = half // HDIM
        self.group = math.gcd(self.heads, 4)
        self.steps = self.heads // self.group
        self.cols = self.group * HDIM
        self.scale = 1.0 / math.sqrt(HDIM)

    def first(self):
        return pl.BlockSpec((self.rows, self.cols), lambda i: (0, i))

    def second(self):
        return pl.BlockSpec((self.rows, self.cols), lambda i: (0, self.steps + i))

    def memory(self, part):
        slots = self.memory_rows // (CAP * BLK)
        return pl.BlockSpec(
            (slots, 2, CAP * BLK, self.cols), lambda i: (0, 0, 0, part * self.steps + i)
        )

    def pair(self):
        return pl.BlockSpec((2 * self.rows, self.cols), lambda i: (0, i))

    def whole(self, shape):
        return pl.BlockSpec(shape, lambda i: (0,) * len(shape))

    def stacked(self):
        return pl.BlockSpec((2, self.rows, self.cols), lambda i: (0, 0, i))


def joined(refs, lanes):
    return jnp.concatenate([ref[:, lanes] for ref in refs], axis=0)


def scores_of(plan, query, key_refs, memory_ref, bias, memory_bias_ref, lanes, rows):
    scaling = plan.scale * LOG2E
    keys = joined(key_refs, lanes)
    current = dot_nt(query, keys) * scaling + bias
    parts, memory_keys = [], []
    for part in range(2):
        mem = memory_ref[:, part, :, lanes].reshape(plan.memory_rows, HDIM)
        score = dot_nt(query[part * rows : (part + 1) * rows], mem)
        parts.append(score * scaling + memory_bias_ref[part : part + 1, :])
        memory_keys.append(mem)
    return keys, memory_keys, current, jnp.concatenate(parts, axis=0)


def widened(column, like):
    return jnp.concatenate([column] * (like.shape[1] // column.shape[1]), axis=1)


def attend_near(plan, own_qd, far_qd, kv, memory, key_row, query_col, memory_bias):
    rows = plan.rows

    def body(qo, qf, k0, k1, v0, v1, mk, mv, krow, qcol, mbias, mixed_out, top_out, total_out):
        bias = visible_bias(krow[0:1, :], krow[1:2, :], qcol[:, 0:1], qcol[:, 1:2])
        for g in range(plan.group):
            lanes = slice(g * HDIM, (g + 1) * HDIM)
            query = joined((qo, qf), lanes)
            _, _, current, mem = scores_of(plan, query, (k0, k1), mk, bias, mbias, lanes, rows)
            top = jnp.maximum(
                jnp.max(current, axis=1, keepdims=True), jnp.max(mem, axis=1, keepdims=True)
            )
            weight = jnp.exp2(current - top)
            mem_weight = jnp.exp2(mem - top)
            total = jnp.sum(weight, axis=1, keepdims=True) + jnp.sum(
                mem_weight, axis=1, keepdims=True
            )
            mixed = dot_nn(weight.astype(BF16), joined((v0, v1), lanes))
            mem16 = mem_weight.astype(BF16)
            mixed_mem = [
                dot_nn(
                    mem16[part * rows : (part + 1) * rows],
                    mv[:, part, :, lanes].reshape(plan.memory_rows, HDIM),
                )
                for part in range(2)
            ]
            mixed_out[:, lanes] = mixed + jnp.concatenate(mixed_mem, axis=0)
            top_out[:, lanes] = jnp.broadcast_to(top, (2 * rows, HDIM))
            total_out[:, lanes] = jnp.broadcast_to(total, (2 * rows, HDIM))

    flops = 2 * 2 * (2 * rows) * (2 * rows + plan.memory_rows) * plan.half
    return pl.pallas_call(
        body,
        grid=(plan.steps,),
        out_shape=(jax.ShapeDtypeStruct((2 * rows, plan.half), F32),) * 3,
        in_specs=[plan.first()] * 4
        + [plan.second()] * 2
        + [plan.memory(0), plan.memory(1)]
        + [plan.whole(key_row.shape), plan.whole(query_col.shape), plan.whole(memory_bias.shape)],
        out_specs=(plan.pair(),) * 3,
        cost_estimate=cost(flops, 12 * rows * plan.half * 2, 2 * rows * 3 * rows * plan.heads),
        compiler_params=pltpu.CompilerParams(vmem_limit_bytes=VMEM_BYTES),
        name="attend_near",
    )(own_qd, far_qd, *kv, *kv, memory, memory, key_row, query_col, memory_bias)


def attend_prev(plan, own_qd, far_qd, kv, key_row, query_col, near):
    rows = plan.rows

    def body(
        qo, qf, do_o, do_f, k0, k1, v0, v1, krow, qcol, mixed_in, top_in, total_in,
        att_own, att_far, level_out, delta_out, stat_row,
    ):
        bias = visible_bias(krow[0:1, :], krow[1:2, :], qcol[:, 0:1], qcol[:, 1:2])
        lane = lax.broadcasted_iota(jnp.int32, (2 * rows, HDIM), 1)
        stats = jnp.zeros((2 * rows, HDIM), F32)
        scaling = plan.scale * LOG2E
        for g in range(plan.group):
            lanes = slice(g * HDIM, (g + 1) * HDIM)
            query = joined((qo, qf), lanes)
            score = dot_nt(query, joined((k0, k1), lanes)) * scaling + bias
            near_top = top_in[:, lanes]
            top = jnp.maximum(
                jnp.broadcast_to(jnp.max(score, axis=1, keepdims=True), near_top.shape), near_top
            )
            weight = jnp.exp2(score - widened(top, score))
            shrink = jnp.exp2(near_top - top)
            total = jnp.sum(weight, axis=1, keepdims=True) + total_in[:, lanes] * shrink
            mixed = dot_nn(weight.astype(BF16), joined((v0, v1), lanes))
            output = (mixed + mixed_in[:, lanes] * shrink) / total
            upstream = joined((do_o, do_f), lanes).astype(F32)
            delta = jnp.sum(upstream * output, axis=1, keepdims=True)
            level = top + jnp.log2(total)
            stats = jnp.where(lane == g, level, stats)
            stats = jnp.where(lane == plan.group + g, delta, stats)
            level_out[:, lanes] = level
            delta_out[:, lanes] = jnp.broadcast_to(delta, level.shape)
            att_own[:, lanes] = output[:rows].astype(BF16)
            att_far[:, lanes] = output[rows:].astype(BF16)
        stat_row[0] = stats.T[0:8, :]

    flops = 2 * 2 * (2 * rows) * (2 * rows) * plan.half
    return pl.pallas_call(
        body,
        grid=(plan.steps,),
        out_shape=(
            jax.ShapeDtypeStruct((rows, plan.half), BF16),
            jax.ShapeDtypeStruct((rows, plan.half), BF16),
            jax.ShapeDtypeStruct((2 * rows, plan.half), F32),
            jax.ShapeDtypeStruct((2 * rows, plan.half), F32),
            jax.ShapeDtypeStruct((plan.steps, 8, 2 * rows), F32),
        ),
        in_specs=[plan.first()] * 2
        + [plan.second()] * 2
        + [plan.first()] * 2
        + [plan.second()] * 2
        + [plan.whole(key_row.shape), plan.whole(query_col.shape)]
        + [plan.pair()] * 3,
        out_specs=(
            plan.first(),
            plan.first(),
            plan.pair(),
            plan.pair(),
            pl.BlockSpec((1, 8, 2 * rows), lambda i: (i, 0, 0)),
        ),
        cost_estimate=cost(flops, 16 * rows * plan.half * 2, 4 * rows * rows * plan.heads),
        compiler_params=pltpu.CompilerParams(vmem_limit_bytes=VMEM_BYTES),
        name="attend_prev",
    )(
        own_qd, far_qd, own_qd, far_qd, *kv, *kv, key_row, query_col, *near
    )


def dot_tn(a, b):
    return lax.dot_general(a, b, (((0,), (0,)), ((), ())), preferred_element_type=F32)


def own_gradients(plan, own_qd, far_qd, kv, memory, key_row, query_col, memory_bias, level, delta):
    rows = plan.rows

    def body(
        qo, qf, do_o, do_f, k0, k1, k2, k3, v0, v1, v2, v3, mk, mv, krow, qcol, mbias,
        level_in, delta_in, dq_own, dq_far, squares, dk, dv,
    ):
        bias = visible_bias(krow[0:1, :], krow[1:2, :], qcol[:, 0:1], qcol[:, 1:2])
        acc = jnp.zeros((8, HDIM), F32)
        for g in range(plan.group):
            lanes = slice(g * HDIM, (g + 1) * HDIM)
            query = joined((qo, qf), lanes)
            upstream = joined((do_o, do_f), lanes)
            level = level_in[:, lanes]
            delta = delta_in[:, lanes]
            keys, mem_keys, current, mem = scores_of(
                plan, query, (k0, k1, k2, k3), mk, bias, mbias, lanes, rows
            )
            values = joined((v0, v1, v2, v3), lanes)
            press = dot_nt(upstream, values) - widened(delta, current)
            prob = jnp.exp2(current - widened(level, current))
            grad = (prob * press).astype(BF16)
            result = dot_nn(grad, keys)
            extra = []
            for part in range(2):
                span = slice(part * rows, (part + 1) * rows)
                mem_values = mv[:, part, :, lanes].reshape(plan.memory_rows, HDIM)
                mem_press = dot_nt(upstream[span], mem_values) - widened(delta[span], mem)
                mem_grad = (jnp.exp2(mem[span] - widened(level[span], mem)) * mem_press).astype(BF16)
                extra.append(dot_nn(mem_grad, mem_keys[part]))
            result = (result + jnp.concatenate(extra, axis=0)) * plan.scale
            dq_own[:, lanes] = result[:rows]
            dq_far[:, lanes] = result[rows:].astype(BF16)
            acc = acc + jnp.sum((result * result).reshape(-1, 8, HDIM), axis=0)
            dk[:, lanes] = dot_tn(grad[:, : 2 * rows], query) * plan.scale
            dv[:, lanes] = dot_tn(prob[:, : 2 * rows].astype(BF16), upstream)

        @pl.when(pl.program_id(0) == 0)
        def _():
            squares[...] = jnp.zeros_like(squares)

        squares[...] += acc

    both = pl.BlockSpec((2 * rows, plan.cols), lambda i: (0, i))
    flops = (3 * (4 * rows + plan.memory_rows) + 4 * rows) * 2 * (2 * rows) * plan.half
    return pl.pallas_call(
        body,
        grid=(plan.steps,),
        out_shape=(
            pltpu.HBM((rows, plan.half), F32),
            jax.ShapeDtypeStruct((rows, plan.half), BF16),
            jax.ShapeDtypeStruct((8, HDIM), F32),
            jax.ShapeDtypeStruct((2 * rows, plan.half), F32),
            jax.ShapeDtypeStruct((2 * rows, plan.half), F32),
        ),
        in_specs=[plan.first()] * 2
        + [plan.second()] * 2
        + [plan.first()] * 4
        + [plan.second()] * 4
        + [plan.memory(0), plan.memory(1)]
        + [plan.whole(key_row.shape), plan.whole(query_col.shape), plan.whole(memory_bias.shape)]
        + [plan.pair()] * 2,
        out_specs=(plan.first(), plan.first(), plan.whole((8, HDIM)), both, both),
        cost_estimate=cost(flops, 22 * rows * plan.half * 2, 2 * rows * 5 * rows * plan.heads),
        compiler_params=pltpu.CompilerParams(vmem_limit_bytes=VMEM_BYTES),
        name="own_gradients",
    )(
        own_qd, far_qd, own_qd, far_qd, *kv, *kv, memory, memory, key_row, query_col, memory_bias,
        level, delta,
    )


def key_terms(plan, key, value, query, upstream, bias, level, delta):
    score = dot_nt(key, query) * (plan.scale * LOG2E) + bias
    prob = jnp.exp2(score - level)
    grad = (prob * (dot_nt(value, upstream) - delta)).astype(BF16)
    return dot_nn(grad, query) * plan.scale, dot_nn(prob.astype(BF16), upstream)


def key_gradient_next(
    plan, own_qd, far_qd, own_kv, far_kv, query_row, key_col, stats, near_dk, near_dv, dq_squares, devices
):
    rows = plan.rows

    def body(
        qo, qf, do_o, do_f, k0, k1, v0, v1, qrow, kcol, stat, dk_in, dv_in, dq_sq,
        dk_own, dv_own, send, share, squares,
    ):
        bias = visible_bias(kcol[:, 0:1], kcol[:, 1:2], qrow[0:1, :], qrow[1:2, :])
        acc = jnp.zeros((8, HDIM), F32)
        for g in range(plan.group):
            lanes = slice(g * HDIM, (g + 1) * HDIM)
            key_part, value_part = key_terms(
                plan,
                joined((k0, k1), lanes),
                joined((v0, v1), lanes),
                joined((qo, qf), lanes),
                joined((do_o, do_f), lanes),
                bias,
                stat[0, g : g + 1, :],
                stat[0, plan.group + g : plan.group + g + 1, :],
            )
            key_part = key_part + dk_in[:, lanes]
            value_part = value_part + dv_in[:, lanes]
            dk_own[:, lanes] = key_part[:rows]
            dv_own[:, lanes] = value_part[:rows]
            send[0, :, lanes] = key_part[rows:].astype(BF16)
            send[1, :, lanes] = value_part[rows:].astype(BF16)
            both = key_part * key_part + value_part * value_part
            acc = acc + jnp.sum(both.reshape(-1, 8, HDIM), axis=0)

        @pl.when(pl.program_id(0) == 0)
        def _():
            squares[...] = dq_sq[...]

        squares[...] += acc

        @pl.when(pl.program_id(0) == plan.steps - 1)
        def _():
            row = jnp.sum(squares[...], axis=0, keepdims=True)
            share[...] = jnp.broadcast_to(row, share.shape)

    both = pl.BlockSpec((2 * rows, plan.cols), lambda i: (0, i))
    return pl.pallas_call(
        body,
        grid=(plan.steps,),
        out_shape=(
            jax.ShapeDtypeStruct((rows, plan.half), F32),
            jax.ShapeDtypeStruct((rows, plan.half), F32),
            jax.ShapeDtypeStruct((2, rows, plan.half), BF16),
            jax.ShapeDtypeStruct((devices, HDIM), F32),
        ),
        in_specs=[plan.first()] * 2
        + [plan.second()] * 2
        + [plan.first()] * 2
        + [plan.second()] * 2
        + [plan.whole(query_row.shape), plan.whole(key_col.shape)]
        + [pl.BlockSpec((1, 8, 2 * rows), lambda i: (i, 0, 0)), both, both]
        + [plan.whole((8, HDIM))],
        out_specs=(plan.first(), plan.first(), plan.stacked(), plan.whole((devices, HDIM))),
        scratch_shapes=[pltpu.VMEM((8, HDIM), F32)],
        cost_estimate=cost(
            4 * 2 * (2 * rows) ** 2 * plan.half, 24 * rows * plan.half * 2, 4 * rows * rows * plan.heads
        ),
        compiler_params=pltpu.CompilerParams(vmem_limit_bytes=VMEM_BYTES),
        name="key_gradient_next",
    )(
        own_qd, far_qd, own_qd, far_qd, own_kv, far_kv, own_kv, far_kv, query_row, key_col, stats,
        near_dk, near_dv, dq_squares,
    )


def scaled(plan, side, shares, entries, dq_own, dq_far, dk_own, dv_own, kv_far):
    rows, half = plan.rows, plan.half

    def body(side_ref, share, dq, dq_other, dk, dv, other, dq_out, dk_out, dv_out):
        squares = jnp.sum(jnp.sum(share[...], axis=0, keepdims=True), axis=1, keepdims=True)
        inverse = 1.0 / jnp.sqrt(squares / entries + 1e-06)
        near = pl.multiple_of(side_ref[0] * half, half)
        away = pl.multiple_of(half - side_ref[0] * half, half)
        for out, mine, theirs in (
            (dq_out, dq[...], dq_other[...]),
            (dk_out, dk[...], other[0]),
            (dv_out, dv[...], other[1]),
        ):
            out[:, pl.ds(near, half)] = (mine * inverse).astype(BF16)
            out[:, pl.ds(away, half)] = (theirs.astype(F32) * inverse).astype(BF16)

    vmem = pl.BlockSpec(memory_space=pltpu.VMEM)
    return pl.pallas_call(
        body,
        out_shape=(jax.ShapeDtypeStruct((rows, 2 * half), BF16),) * 3,
        in_specs=[pl.BlockSpec(memory_space=pltpu.SMEM)] + [vmem] * 6,
        out_specs=(vmem,) * 3,
        cost_estimate=cost(6 * rows * half, 20 * rows * half),
        compiler_params=pltpu.CompilerParams(vmem_limit_bytes=VMEM_BYTES),
        name="scaled",
    )(side, shares, dq_own, dq_far, dk_own, dv_own, kv_far)


def on_device(query, keys, values, memory_keys, memory_values, routes, documents, cotangent):
    rows, width = query.shape
    half = width // 2
    count = lax.axis_size("ctx")
    devices = count * lax.axis_size("head")
    position = lax.axis_index("ctx").astype(jnp.int32)
    side = position % 2
    partner = position + 1 - 2 * side
    per_device = memory_keys.shape[0] // BLK
    memory_rows = count * CAP * BLK
    plan = Plan(rows, half, memory_rows)

    packed = pack_memory(position, routes, memory_keys, memory_values, count)
    own_kv, sent_kv = halves(position, keys, values)
    own_qd, sent_qd = halves(position, query, cotangent)
    far_kv = swapped(sent_kv)
    prev_own_kv = shifted(own_kv, 2)
    next_own_qd = shifted(own_qd, -2)
    far_kv, sent_qd = lax.optimization_barrier((far_kv, sent_qd))
    prev_far_kv = shifted(far_kv, 2)
    far_qd = swapped(sent_qd)
    route_table = routes[:, 0].reshape(count, per_device)
    arrived = lax.all_to_all(
        packed.reshape(count, 2 * CAP * BLK, width), "ctx", split_axis=0, concat_axis=0, tiled=True
    ).reshape(count, 2, CAP * BLK, width)

    def labels(block):
        docs = lax.dynamic_slice_in_dim(documents, block * rows, rows)
        docs = jnp.where((block >= 0) & (block < count), docs, -1)
        return jnp.stack([docs, block * rows + jnp.arange(rows, dtype=jnp.int32)])

    near_row = jnp.concatenate([labels(position), labels(partner)], axis=1)
    prev_row = jnp.concatenate([labels(position - 2), labels(partner - 2)], axis=1)
    next_row = jnp.concatenate([labels(position + 2), labels(partner + 2)], axis=1)
    key_row = jnp.concatenate([near_row, prev_row], axis=1)
    near_col = near_row.T
    readers = jnp.stack([position, partner])
    arrivals = jnp.sum((route_table[None] == readers[:, None, None]).astype(jnp.int32), axis=2)
    live = jnp.arange(CAP, dtype=jnp.int32)[None, None, :] < arrivals[:, :, None]
    memory_bias = jnp.broadcast_to(
        jnp.where(live, 0.0, NEGATIVE)[..., None], (2, count, CAP, BLK)
    ).reshape(2, memory_rows)

    far_qd, near_row, prev_row, next_row, key_row, near_col, memory_bias = lax.optimization_barrier(
        (far_qd, near_row, prev_row, next_row, key_row, near_col, memory_bias)
    )
    next_far_qd = shifted(far_qd, -2)
    kv = (own_kv, far_kv, prev_own_kv, prev_far_kv)
    near = attend_near(plan, own_qd, far_qd, kv[:2], arrived, near_row, near_col, memory_bias)
    att_own, att_far, level, delta, stat_row = attend_prev(
        plan, own_qd, far_qd, kv[2:], prev_row, near_col, near
    )
    next_stats = shifted(stat_row, -2)
    att_back = swapped(att_far)
    dq_own, dq_far, dq_squares, near_dk, near_dv = own_gradients(
        plan, own_qd, far_qd, kv, arrived, key_row, near_col, memory_bias, level, delta
    )
    next_stats, dq_far, att_back = lax.optimization_barrier((next_stats, dq_far, att_back))
    dq_back = swapped(dq_far)
    dk_own, dv_own, second_send, share = key_gradient_next(
        plan, next_own_qd, next_far_qd, own_kv, far_kv, next_row, near_col, next_stats,
        near_dk, near_dv, dq_squares, devices,
    )
    second_send, dq_back = lax.optimization_barrier((second_send, dq_back))
    second_back = swapped(second_send)
    shares = lax.all_to_all(share, ("ctx", "head"), split_axis=0, concat_axis=0, tiled=True)
    entries = 3.0 * count * rows * width * lax.axis_size("head")
    query_grad, key_grad, value_grad = scaled(
        plan, side[None], shares, entries, dq_own, dq_back, dk_own, dv_own, second_back
    )
    attended = jnp.where(
        side == 0,
        jnp.concatenate([att_own, att_back], axis=1),
        jnp.concatenate([att_back, att_own], axis=1),
    )
    return attended, query_grad, key_grad, value_grad


def solution(mesh):
    spread = P("ctx", "head")
    return jax.shard_map(
        on_device,
        mesh=mesh,
        in_specs=(spread,) * 5 + (P(), P(), spread),
        out_specs=(spread,) * 4,
        check_vma=False,
    )
```

```python
import math

import jax
import jax.numpy as jnp
from jax import lax
from jax.experimental import pallas as pl
from jax.experimental.pallas import tpu as pltpu
from jax.sharding import PartitionSpec as P

HDIM = 128
BLK = 8
CAP = 2
NEGATIVE = -1e30
LOG2E = 1.4426950408889634
F32 = jnp.float32
BF16 = jnp.bfloat16
VMEM_BYTES = 20 * 2**20


def dot_nt(a, b):
    return lax.dot_general(a, b, (((1,), (1,)), ((), ())), preferred_element_type=F32)


def dot_nn(a, b):
    return lax.dot_general(a, b, (((1,), (0,)), ((), ())), preferred_element_type=F32)


def shifted(value, steps):
    count = lax.axis_size("ctx")
    pairs = [(i, i + steps) for i in range(count) if 0 <= i + steps < count]
    return lax.ppermute(value, "ctx", pairs)


def swapped(value):
    count = lax.axis_size("ctx")
    return lax.ppermute(value, "ctx", [(i, i ^ 1) for i in range(count)])


def cost(flops, size, exps=0):
    return pl.CostEstimate(flops=int(flops), bytes_accessed=int(size), transcendentals=int(exps))


def halves(position, left, right):
    rows, width = left.shape
    half = width // 2

    def body(where, one, two, kept, sent, sems):
        side = where[0] % 2
        near = pl.ds(pl.multiple_of(side * half, half), half)
        away = pl.ds(pl.multiple_of(half - side * half, half), half)
        cuts = [(away, sent), (near, kept)]
        copies = []
        for n, (cols, out) in enumerate(cuts):
            for m, src in enumerate((one, two)):
                dst = out.at[:, pl.ds(m * half, half)]
                copies.append(pltpu.make_async_copy(src.at[:, cols], dst, sems.at[n, m]))
        for copy in copies:
            copy.start()
        for copy in copies:
            copy.wait()

    hbm = pl.BlockSpec(memory_space=pltpu.HBM)
    return pl.pallas_call(
        body,
        out_shape=(jax.ShapeDtypeStruct((rows, width), BF16),) * 2,
        in_specs=[pl.BlockSpec(memory_space=pltpu.SMEM), hbm, hbm],
        out_specs=(pl.BlockSpec(memory_space=pltpu.VMEM),) * 2,
        scratch_shapes=[pltpu.SemaphoreType.DMA((2, 2))],
        cost_estimate=cost(0, 4 * rows * width * 2),
        compiler_params=pltpu.CompilerParams(vmem_limit_bytes=60 * 2**20),
        name="halves",
    )(position[None], left, right)


def pack_memory(position, routes, memory_keys, memory_values, count):
    blocks = memory_keys.shape[0] // BLK
    width = memory_keys.shape[1]
    half = width // 2

    def body(where, routes_ref, mk, mv, packed, keys, values, used, sems):
        copies = [
            pltpu.make_async_copy(mk, keys, sems.at[0]),
            pltpu.make_async_copy(mv, values, sems.at[1]),
        ]
        for copy in copies:
            copy.start()
        packed[...] = jnp.zeros_like(packed)
        for owner in range(count):
            used[owner] = 0
        for copy in copies:
            copy.wait()

        def place(block, carry):
            owner = routes_ref[where[0] * blocks + block]
            slot = used[owner]
            used[owner] = slot + 1
            odd = owner % 2
            partner = owner + 1 - 2 * odd
            near = pl.ds(pl.multiple_of(odd * half, half), half)
            away = pl.ds(pl.multiple_of(half - odd * half, half), half)
            packed[owner, 0, slot, :, :half] = keys[block, :, near]
            packed[owner, 0, slot, :, half:] = values[block, :, near]
            packed[partner, 1, slot, :, :half] = keys[block, :, away]
            packed[partner, 1, slot, :, half:] = values[block, :, away]
            return carry

        lax.fori_loop(0, blocks, place, 0)

    smem = pl.BlockSpec(memory_space=pltpu.SMEM)
    hbm = pl.BlockSpec(memory_space=pltpu.HBM)
    return pl.pallas_call(
        body,
        out_shape=jax.ShapeDtypeStruct((count, 2, CAP, BLK, width), BF16),
        in_specs=[smem, smem, hbm, hbm],
        out_specs=pl.BlockSpec(memory_space=pltpu.VMEM),
        scratch_shapes=[
            pltpu.VMEM((blocks, BLK, width), BF16),
            pltpu.VMEM((blocks, BLK, width), BF16),
            pltpu.SMEM((count,), jnp.int32),
            pltpu.SemaphoreType.DMA((2,)),
        ],
        cost_estimate=cost(0, 4 * memory_keys.size * 2),
        compiler_params=pltpu.CompilerParams(vmem_limit_bytes=60 * 2**20),
        name="pack_memory",
    )(
        position[None],
        routes.reshape(-1),
        memory_keys.reshape(blocks, BLK, width),
        memory_values.reshape(blocks, BLK, width),
    )


def visible_bias(key_doc, key_pos, query_doc, query_pos):
    return jnp.where((key_doc == query_doc) & (key_pos <= query_pos), 0.0, NEGATIVE)


class Plan:
    def __init__(self, rows, half, memory_rows):
        self.rows, self.half, self.memory_rows = rows, half, memory_rows
        self.heads = half // HDIM
        self.group = math.gcd(self.heads, 4)
        self.steps = self.heads // self.group
        self.cols = self.group * HDIM
        self.scale = 1.0 / math.sqrt(HDIM)

    def first(self):
        return pl.BlockSpec((self.rows, self.cols), lambda i: (0, i))

    def second(self):
        return pl.BlockSpec((self.rows, self.cols), lambda i: (0, self.steps + i))

    def memory(self, part):
        slots = self.memory_rows // (CAP * BLK)
        return pl.BlockSpec(
            (slots, 2, CAP * BLK, self.cols), lambda i: (0, 0, 0, part * self.steps + i)
        )

    def pair(self):
        return pl.BlockSpec((2 * self.rows, self.cols), lambda i: (0, i))

    def whole(self, shape):
        return pl.BlockSpec(shape, lambda i: (0,) * len(shape))

    def stacked(self):
        return pl.BlockSpec((2, self.rows, self.cols), lambda i: (0, 0, i))


def joined(refs, lanes):
    return jnp.concatenate([ref[:, lanes] for ref in refs], axis=0)


def scores_of(plan, query, key_refs, memory_ref, bias, memory_bias_ref, lanes, rows):
    scaling = plan.scale * LOG2E
    keys = joined(key_refs, lanes)
    current = dot_nt(query, keys) * scaling + bias
    parts, memory_keys = [], []
    for part in range(2):
        mem = memory_ref[:, part, :, lanes].reshape(plan.memory_rows, HDIM)
        score = dot_nt(query[part * rows : (part + 1) * rows], mem)
        parts.append(score * scaling + memory_bias_ref[part : part + 1, :])
        memory_keys.append(mem)
    return keys, memory_keys, current, jnp.concatenate(parts, axis=0)


def widened(column, like):
    return jnp.concatenate([column] * (like.shape[1] // column.shape[1]), axis=1)


def attend_near(plan, own_qd, far_qd, kv, memory, key_row, query_col, memory_bias, token):
    rows = plan.rows

    def body(qo, qf, k0, k1, v0, v1, mk, mv, krow, qcol, mbias, _, mixed_out, top_out, total_out):
        bias = visible_bias(krow[0:1, :], krow[1:2, :], qcol[:, 0:1], qcol[:, 1:2])
        for g in range(plan.group):
            lanes = slice(g * HDIM, (g + 1) * HDIM)
            query = joined((qo, qf), lanes)
            _, _, current, mem = scores_of(plan, query, (k0, k1), mk, bias, mbias, lanes, rows)
            top = jnp.maximum(
                jnp.max(current, axis=1, keepdims=True), jnp.max(mem, axis=1, keepdims=True)
            )
            weight = jnp.exp2(current - top)
            mem_weight = jnp.exp2(mem - top)
            total = jnp.sum(weight, axis=1, keepdims=True) + jnp.sum(
                mem_weight, axis=1, keepdims=True
            )
            mixed = dot_nn(weight.astype(BF16), joined((v0, v1), lanes))
            mem16 = mem_weight.astype(BF16)
            mixed_mem = [
                dot_nn(
                    mem16[part * rows : (part + 1) * rows],
                    mv[:, part, :, lanes].reshape(plan.memory_rows, HDIM),
                )
                for part in range(2)
            ]
            mixed_out[:, lanes] = mixed + jnp.concatenate(mixed_mem, axis=0)
            top_out[:, lanes] = jnp.broadcast_to(top, (2 * rows, HDIM))
            total_out[:, lanes] = jnp.broadcast_to(total, (2 * rows, HDIM))

    flops = 2 * 2 * (2 * rows) * (2 * rows + plan.memory_rows) * plan.half
    return pl.pallas_call(
        body,
        grid=(plan.steps,),
        out_shape=(jax.ShapeDtypeStruct((2 * rows, plan.half), F32),) * 3,
        in_specs=[plan.first()] * 4
        + [plan.second()] * 2
        + [plan.memory(0), plan.memory(1)]
        + [plan.whole(key_row.shape), plan.whole(query_col.shape), plan.whole(memory_bias.shape)]
        + [plan.whole(token.shape)],
        out_specs=(plan.pair(),) * 3,
        cost_estimate=cost(flops, 12 * rows * plan.half * 2, 2 * rows * 3 * rows * plan.heads),
        compiler_params=pltpu.CompilerParams(vmem_limit_bytes=VMEM_BYTES),
        name="attend_near",
    )(own_qd, far_qd, *kv, *kv, memory, memory, key_row, query_col, memory_bias, token)


def attend_prev(plan, own_qd, far_qd, kv, key_row, query_col, near):
    rows = plan.rows

    def body(
        qo, qf, do_o, do_f, k0, k1, v0, v1, krow, qcol, mixed_in, top_in, total_in,
        att_own, att_far, level_out, delta_out, stat_row,
    ):
        bias = visible_bias(krow[0:1, :], krow[1:2, :], qcol[:, 0:1], qcol[:, 1:2])
        lane = lax.broadcasted_iota(jnp.int32, (2 * rows, HDIM), 1)
        stats = jnp.zeros((2 * rows, HDIM), F32)
        scaling = plan.scale * LOG2E
        for g in range(plan.group):
            lanes = slice(g * HDIM, (g + 1) * HDIM)
            query = joined((qo, qf), lanes)
            score = dot_nt(query, joined((k0, k1), lanes)) * scaling + bias
            near_top = top_in[:, lanes]
            top = jnp.maximum(
                jnp.broadcast_to(jnp.max(score, axis=1, keepdims=True), near_top.shape), near_top
            )
            weight = jnp.exp2(score - widened(top, score))
            shrink = jnp.exp2(near_top - top)
            total = jnp.sum(weight, axis=1, keepdims=True) + total_in[:, lanes] * shrink
            mixed = dot_nn(weight.astype(BF16), joined((v0, v1), lanes))
            output = (mixed + mixed_in[:, lanes] * shrink) / total
            upstream = joined((do_o, do_f), lanes).astype(F32)
            delta = jnp.sum(upstream * output, axis=1, keepdims=True)
            level = top + jnp.log2(total)
            stats = jnp.where(lane == g, level, stats)
            stats = jnp.where(lane == plan.group + g, delta, stats)
            level_out[:, lanes] = level
            delta_out[:, lanes] = jnp.broadcast_to(delta, level.shape)
            att_own[:, lanes] = output[:rows].astype(BF16)
            att_far[:, lanes] = output[rows:].astype(BF16)
        stat_row[0] = stats.T[0:8, :]

    flops = 2 * 2 * (2 * rows) * (2 * rows) * plan.half
    return pl.pallas_call(
        body,
        grid=(plan.steps,),
        out_shape=(
            jax.ShapeDtypeStruct((rows, plan.half), BF16),
            jax.ShapeDtypeStruct((rows, plan.half), BF16),
            jax.ShapeDtypeStruct((2 * rows, plan.half), F32),
            jax.ShapeDtypeStruct((2 * rows, plan.half), F32),
            jax.ShapeDtypeStruct((plan.steps, 8, 2 * rows), F32),
        ),
        in_specs=[plan.first()] * 2
        + [plan.second()] * 2
        + [plan.first()] * 2
        + [plan.second()] * 2
        + [plan.whole(key_row.shape), plan.whole(query_col.shape)]
        + [plan.pair()] * 3,
        out_specs=(
            plan.first(),
            plan.first(),
            plan.pair(),
            plan.pair(),
            pl.BlockSpec((1, 8, 2 * rows), lambda i: (i, 0, 0)),
        ),
        cost_estimate=cost(flops, 16 * rows * plan.half * 2, 4 * rows * rows * plan.heads),
        compiler_params=pltpu.CompilerParams(vmem_limit_bytes=VMEM_BYTES),
        name="attend_prev",
    )(
        own_qd, far_qd, own_qd, far_qd, *kv, *kv, key_row, query_col, *near
    )


def dot_tn(a, b):
    return lax.dot_general(a, b, (((0,), (0,)), ((), ())), preferred_element_type=F32)


def own_gradients(plan, own_qd, far_qd, kv, memory, key_row, query_col, memory_bias, level, delta):
    rows = plan.rows

    def body(
        qo, qf, do_o, do_f, k0, k1, k2, k3, v0, v1, v2, v3, mk, mv, krow, qcol, mbias,
        level_in, delta_in, dq_own, dq_far, squares, dk, dv,
    ):
        bias = visible_bias(krow[0:1, :], krow[1:2, :], qcol[:, 0:1], qcol[:, 1:2])
        acc = jnp.zeros((8, HDIM), F32)
        for g in range(plan.group):
            lanes = slice(g * HDIM, (g + 1) * HDIM)
            query = joined((qo, qf), lanes)
            upstream = joined((do_o, do_f), lanes)
            level = level_in[:, lanes]
            delta = delta_in[:, lanes]
            keys, mem_keys, current, mem = scores_of(
                plan, query, (k0, k1, k2, k3), mk, bias, mbias, lanes, rows
            )
            values = joined((v0, v1, v2, v3), lanes)
            press = dot_nt(upstream, values) - widened(delta, current)
            prob = jnp.exp2(current - widened(level, current))
            grad = (prob * press).astype(BF16)
            result = dot_nn(grad, keys)
            extra = []
            for part in range(2):
                span = slice(part * rows, (part + 1) * rows)
                mem_values = mv[:, part, :, lanes].reshape(plan.memory_rows, HDIM)
                mem_press = dot_nt(upstream[span], mem_values) - widened(delta[span], mem)
                mem_grad = (jnp.exp2(mem[span] - widened(level[span], mem)) * mem_press).astype(BF16)
                extra.append(dot_nn(mem_grad, mem_keys[part]))
            result = (result + jnp.concatenate(extra, axis=0)) * plan.scale
            dq_own[:, lanes] = result[:rows]
            dq_far[:, lanes] = result[rows:].astype(BF16)
            acc = acc + jnp.sum((result * result).reshape(-1, 8, HDIM), axis=0)
            dk[:, lanes] = dot_tn(grad[:, : 2 * rows], query) * plan.scale
            dv[:, lanes] = dot_tn(prob[:, : 2 * rows].astype(BF16), upstream)

        @pl.when(pl.program_id(0) == 0)
        def _():
            squares[...] = jnp.zeros_like(squares)

        squares[...] += acc

    both = pl.BlockSpec((2 * rows, plan.cols), lambda i: (0, i))
    flops = (3 * (4 * rows + plan.memory_rows) + 4 * rows) * 2 * (2 * rows) * plan.half
    return pl.pallas_call(
        body,
        grid=(plan.steps,),
        out_shape=(
            pltpu.HBM((rows, plan.half), F32),
            jax.ShapeDtypeStruct((rows, plan.half), BF16),
            jax.ShapeDtypeStruct((8, HDIM), F32),
            jax.ShapeDtypeStruct((2 * rows, plan.half), F32),
            jax.ShapeDtypeStruct((2 * rows, plan.half), F32),
        ),
        in_specs=[plan.first()] * 2
        + [plan.second()] * 2
        + [plan.first()] * 4
        + [plan.second()] * 4
        + [plan.memory(0), plan.memory(1)]
        + [plan.whole(key_row.shape), plan.whole(query_col.shape), plan.whole(memory_bias.shape)]
        + [plan.pair()] * 2,
        out_specs=(plan.first(), plan.first(), plan.whole((8, HDIM)), both, both),
        cost_estimate=cost(flops, 22 * rows * plan.half * 2, 2 * rows * 5 * rows * plan.heads),
        compiler_params=pltpu.CompilerParams(vmem_limit_bytes=VMEM_BYTES),
        name="own_gradients",
    )(
        own_qd, far_qd, own_qd, far_qd, *kv, *kv, memory, memory, key_row, query_col, memory_bias,
        level, delta,
    )


def key_terms(plan, key, value, query, upstream, bias, level, delta):
    score = dot_nt(key, query) * (plan.scale * LOG2E) + bias
    prob = jnp.exp2(score - level)
    grad = (prob * (dot_nt(value, upstream) - delta)).astype(BF16)
    return dot_nn(grad, query) * plan.scale, dot_nn(prob.astype(BF16), upstream)


def key_gradient_next(
    plan, own_qd, far_qd, own_kv, far_kv, query_row, key_col, stats, near_dk, near_dv, dq_squares, devices
):
    rows = plan.rows

    def body(
        qo, qf, do_o, do_f, k0, k1, v0, v1, qrow, kcol, stat, dk_in, dv_in, dq_sq,
        dk_own, dv_own, send, share, squares,
    ):
        bias = visible_bias(kcol[:, 0:1], kcol[:, 1:2], qrow[0:1, :], qrow[1:2, :])
        acc = jnp.zeros((8, HDIM), F32)
        for g in range(plan.group):
            lanes = slice(g * HDIM, (g + 1) * HDIM)
            key_part, value_part = key_terms(
                plan,
                joined((k0, k1), lanes),
                joined((v0, v1), lanes),
                joined((qo, qf), lanes),
                joined((do_o, do_f), lanes),
                bias,
                stat[0, g : g + 1, :],
                stat[0, plan.group + g : plan.group + g + 1, :],
            )
            key_part = key_part + dk_in[:, lanes]
            value_part = value_part + dv_in[:, lanes]
            dk_own[:, lanes] = key_part[:rows]
            dv_own[:, lanes] = value_part[:rows]
            send[0, :, lanes] = key_part[rows:].astype(BF16)
            send[1, :, lanes] = value_part[rows:].astype(BF16)
            both = key_part * key_part + value_part * value_part
            acc = acc + jnp.sum(both.reshape(-1, 8, HDIM), axis=0)

        @pl.when(pl.program_id(0) == 0)
        def _():
            squares[...] = dq_sq[...]

        squares[...] += acc

        @pl.when(pl.program_id(0) == plan.steps - 1)
        def _():
            row = jnp.sum(squares[...], axis=0, keepdims=True)
            share[...] = jnp.broadcast_to(row, share.shape)

    both = pl.BlockSpec((2 * rows, plan.cols), lambda i: (0, i))
    return pl.pallas_call(
        body,
        grid=(plan.steps,),
        out_shape=(
            jax.ShapeDtypeStruct((rows, plan.half), F32),
            jax.ShapeDtypeStruct((rows, plan.half), F32),
            jax.ShapeDtypeStruct((2, rows, plan.half), BF16),
            jax.ShapeDtypeStruct((devices, HDIM), F32),
        ),
        in_specs=[plan.first()] * 2
        + [plan.second()] * 2
        + [plan.first()] * 2
        + [plan.second()] * 2
        + [plan.whole(query_row.shape), plan.whole(key_col.shape)]
        + [pl.BlockSpec((1, 8, 2 * rows), lambda i: (i, 0, 0)), both, both]
        + [plan.whole((8, HDIM))],
        out_specs=(plan.first(), plan.first(), plan.stacked(), plan.whole((devices, HDIM))),
        scratch_shapes=[pltpu.VMEM((8, HDIM), F32)],
        cost_estimate=cost(
            4 * 2 * (2 * rows) ** 2 * plan.half, 24 * rows * plan.half * 2, 4 * rows * rows * plan.heads
        ),
        compiler_params=pltpu.CompilerParams(vmem_limit_bytes=VMEM_BYTES),
        name="key_gradient_next",
    )(
        own_qd, far_qd, own_qd, far_qd, own_kv, far_kv, own_kv, far_kv, query_row, key_col, stats,
        near_dk, near_dv, dq_squares,
    )


def scaled(plan, side, shares, entries, dq_own, dq_far, dk_own, dv_own, kv_far):
    rows, half = plan.rows, plan.half

    def body(side_ref, share, dq, dq_other, dk, dv, other, dq_out, dk_out, dv_out):
        squares = jnp.sum(jnp.sum(share[...], axis=0, keepdims=True), axis=1, keepdims=True)
        inverse = 1.0 / jnp.sqrt(squares / entries + 1e-06)
        near = pl.multiple_of(side_ref[0] * half, half)
        away = pl.multiple_of(half - side_ref[0] * half, half)
        for out, mine, theirs in (
            (dq_out, dq[...], dq_other[...]),
            (dk_out, dk[...], other[0]),
            (dv_out, dv[...], other[1]),
        ):
            out[:, pl.ds(near, half)] = (mine * inverse).astype(BF16)
            out[:, pl.ds(away, half)] = (theirs.astype(F32) * inverse).astype(BF16)

    vmem = pl.BlockSpec(memory_space=pltpu.VMEM)
    return pl.pallas_call(
        body,
        out_shape=(jax.ShapeDtypeStruct((rows, 2 * half), BF16),) * 3,
        in_specs=[pl.BlockSpec(memory_space=pltpu.SMEM)] + [vmem] * 6,
        out_specs=(vmem,) * 3,
        cost_estimate=cost(6 * rows * half, 20 * rows * half),
        compiler_params=pltpu.CompilerParams(vmem_limit_bytes=VMEM_BYTES),
        name="scaled",
    )(side, shares, dq_own, dq_far, dk_own, dv_own, kv_far)


def on_device(query, keys, values, memory_keys, memory_values, routes, documents, cotangent):
    rows, width = query.shape
    half = width // 2
    count = lax.axis_size("ctx")
    devices = count * lax.axis_size("head")
    position = lax.axis_index("ctx").astype(jnp.int32)
    side = position % 2
    partner = position + 1 - 2 * side
    per_device = memory_keys.shape[0] // BLK
    memory_rows = count * CAP * BLK
    plan = Plan(rows, half, memory_rows)

    packed = pack_memory(position, routes, memory_keys, memory_values, count)
    own_kv, sent_kv = halves(position, keys, values)
    own_qd, sent_qd = halves(position, query, cotangent)
    far_kv = swapped(sent_kv)
    prev_own_kv = shifted(own_kv, 2)
    next_own_qd = shifted(own_qd, -2)
    token = prev_own_kv[:8, :128] + far_kv[:8, :128]
    for _ in range(5):
        token = lax.ppermute(token, "head", [(i, i ^ 1) for i in range(lax.axis_size("head"))])
    far_kv, sent_qd = lax.optimization_barrier((far_kv, sent_qd))
    relayed_kv, token = lax.optimization_barrier((far_kv, token))
    prev_far_kv = shifted(relayed_kv, 2)
    far_qd = swapped(sent_qd)
    route_table = routes[:, 0].reshape(count, per_device)
    arrived = lax.all_to_all(
        packed.reshape(count, 2 * CAP * BLK, width), "ctx", split_axis=0, concat_axis=0, tiled=True
    ).reshape(count, 2, CAP * BLK, width)

    def labels(block):
        docs = lax.dynamic_slice_in_dim(documents, block * rows, rows)
        docs = jnp.where((block >= 0) & (block < count), docs, -1)
        return jnp.stack([docs, block * rows + jnp.arange(rows, dtype=jnp.int32)])

    near_row = jnp.concatenate([labels(position), labels(partner)], axis=1)
    prev_row = jnp.concatenate([labels(position - 2), labels(partner - 2)], axis=1)
    next_row = jnp.concatenate([labels(position + 2), labels(partner + 2)], axis=1)
    key_row = jnp.concatenate([near_row, prev_row], axis=1)
    near_col = near_row.T
    readers = jnp.stack([position, partner])
    arrivals = jnp.sum((route_table[None] == readers[:, None, None]).astype(jnp.int32), axis=2)
    live = jnp.arange(CAP, dtype=jnp.int32)[None, None, :] < arrivals[:, :, None]
    memory_bias = jnp.broadcast_to(
        jnp.where(live, 0.0, NEGATIVE)[..., None], (2, count, CAP, BLK)
    ).reshape(2, memory_rows)

    far_qd, near_row, prev_row, next_row, key_row, near_col, memory_bias = lax.optimization_barrier(
        (far_qd, near_row, prev_row, next_row, key_row, near_col, memory_bias)
    )
    next_far_qd = shifted(far_qd, -2)
    kv = (own_kv, far_kv, prev_own_kv, prev_far_kv)
    near = attend_near(plan, own_qd, far_qd, kv[:2], arrived, near_row, near_col, memory_bias, token)
    att_own, att_far, level, delta, stat_row = attend_prev(
        plan, own_qd, far_qd, kv[2:], prev_row, near_col, near
    )
    next_stats = shifted(stat_row, -2)
    att_back = swapped(att_far)
    dq_own, dq_far, dq_squares, near_dk, near_dv = own_gradients(
        plan, own_qd, far_qd, kv, arrived, key_row, near_col, memory_bias, level, delta
    )
    next_stats, dq_far, att_back = lax.optimization_barrier((next_stats, dq_far, att_back))
    dq_back = swapped(dq_far)
    dk_own, dv_own, second_send, share = key_gradient_next(
        plan, next_own_qd, next_far_qd, own_kv, far_kv, next_row, near_col, next_stats,
        near_dk, near_dv, dq_squares, devices,
    )
    second_send, dq_back = lax.optimization_barrier((second_send, dq_back))
    second_back = swapped(second_send)
    shares = lax.all_to_all(share, ("ctx", "head"), split_axis=0, concat_axis=0, tiled=True)
    entries = 3.0 * count * rows * width * lax.axis_size("head")
    query_grad, key_grad, value_grad = scaled(
        plan, side[None], shares, entries, dq_own, dq_back, dk_own, dv_own, second_back
    )
    attended = jnp.where(
        side == 0,
        jnp.concatenate([att_own, att_back], axis=1),
        jnp.concatenate([att_back, att_own], axis=1),
    )
    return attended, query_grad, key_grad, value_grad


def solution(mesh):
    spread = P("ctx", "head")
    return jax.shard_map(
        on_device,
        mesh=mesh,
        in_specs=(spread,) * 5 + (P(), P(), spread),
        out_specs=(spread,) * 4,
        check_vma=False,
    )
```

```python
import math

import jax
import jax.numpy as jnp
from jax import lax
from jax.experimental import pallas as pl
from jax.experimental.pallas import tpu as pltpu
from jax.sharding import PartitionSpec as P

HDIM = 128
BLK = 8
CAP = 2
NEGATIVE = -1e30
LOG2E = 1.4426950408889634
F32 = jnp.float32
BF16 = jnp.bfloat16
VMEM_BYTES = 20 * 2**20


def dot_nt(a, b):
    return lax.dot_general(a, b, (((1,), (1,)), ((), ())), preferred_element_type=F32)


def dot_nn(a, b):
    return lax.dot_general(a, b, (((1,), (0,)), ((), ())), preferred_element_type=F32)


def shifted(value, steps):
    count = lax.axis_size("ctx")
    pairs = [(i, i + steps) for i in range(count) if 0 <= i + steps < count]
    return lax.ppermute(value, "ctx", pairs)


def swapped(value):
    count = lax.axis_size("ctx")
    return lax.ppermute(value, "ctx", [(i, i ^ 1) for i in range(count)])


def cost(flops, size, exps=0):
    return pl.CostEstimate(flops=int(flops), bytes_accessed=int(size), transcendentals=int(exps))


def halves(position, left, right):
    rows, width = left.shape
    half = width // 2

    def body(where, one, two, kept, sent, sems):
        side = where[0] % 2
        near = pl.ds(pl.multiple_of(side * half, half), half)
        away = pl.ds(pl.multiple_of(half - side * half, half), half)
        cuts = [(away, sent), (near, kept)]
        copies = []
        for n, (cols, out) in enumerate(cuts):
            for m, src in enumerate((one, two)):
                dst = out.at[:, pl.ds(m * half, half)]
                copies.append(pltpu.make_async_copy(src.at[:, cols], dst, sems.at[n, m]))
        for copy in copies:
            copy.start()
        for copy in copies:
            copy.wait()

    hbm = pl.BlockSpec(memory_space=pltpu.HBM)
    return pl.pallas_call(
        body,
        out_shape=(jax.ShapeDtypeStruct((rows, width), BF16),) * 2,
        in_specs=[pl.BlockSpec(memory_space=pltpu.SMEM), hbm, hbm],
        out_specs=(pl.BlockSpec(memory_space=pltpu.VMEM),) * 2,
        scratch_shapes=[pltpu.SemaphoreType.DMA((2, 2))],
        cost_estimate=cost(0, 4 * rows * width * 2),
        compiler_params=pltpu.CompilerParams(vmem_limit_bytes=60 * 2**20),
        name="halves",
    )(position[None], left, right)


def pack_memory(position, routes, memory_keys, memory_values, count):
    blocks = memory_keys.shape[0] // BLK
    width = memory_keys.shape[1]
    half = width // 2

    def body(where, routes_ref, mk, mv, packed, keys, values, used, sems):
        copies = [
            pltpu.make_async_copy(mk, keys, sems.at[0]),
            pltpu.make_async_copy(mv, values, sems.at[1]),
        ]
        for copy in copies:
            copy.start()
        packed[...] = jnp.zeros_like(packed)
        for owner in range(count):
            used[owner] = 0
        for copy in copies:
            copy.wait()

        def place(block, carry):
            owner = routes_ref[where[0] * blocks + block]
            slot = used[owner]
            used[owner] = slot + 1
            odd = owner % 2
            partner = owner + 1 - 2 * odd
            near = pl.ds(pl.multiple_of(odd * half, half), half)
            away = pl.ds(pl.multiple_of(half - odd * half, half), half)
            packed[owner, 0, slot, :, :half] = keys[block, :, near]
            packed[owner, 0, slot, :, half:] = values[block, :, near]
            packed[partner, 1, slot, :, :half] = keys[block, :, away]
            packed[partner, 1, slot, :, half:] = values[block, :, away]
            return carry

        lax.fori_loop(0, blocks, place, 0)

    smem = pl.BlockSpec(memory_space=pltpu.SMEM)
    hbm = pl.BlockSpec(memory_space=pltpu.HBM)
    return pl.pallas_call(
        body,
        out_shape=jax.ShapeDtypeStruct((count, 2, CAP, BLK, width), BF16),
        in_specs=[smem, smem, hbm, hbm],
        out_specs=pl.BlockSpec(memory_space=pltpu.VMEM),
        scratch_shapes=[
            pltpu.VMEM((blocks, BLK, width), BF16),
            pltpu.VMEM((blocks, BLK, width), BF16),
            pltpu.SMEM((count,), jnp.int32),
            pltpu.SemaphoreType.DMA((2,)),
        ],
        cost_estimate=cost(0, 4 * memory_keys.size * 2),
        compiler_params=pltpu.CompilerParams(vmem_limit_bytes=60 * 2**20),
        name="pack_memory",
    )(
        position[None],
        routes.reshape(-1),
        memory_keys.reshape(blocks, BLK, width),
        memory_values.reshape(blocks, BLK, width),
    )


def visible_bias(key_doc, key_pos, query_doc, query_pos):
    return jnp.where((key_doc == query_doc) & (key_pos <= query_pos), 0.0, NEGATIVE)


class Plan:
    def __init__(self, rows, half, memory_rows):
        self.rows, self.half, self.memory_rows = rows, half, memory_rows
        self.heads = half // HDIM
        self.group = math.gcd(self.heads, 4)
        self.steps = self.heads // self.group
        self.cols = self.group * HDIM
        self.scale = 1.0 / math.sqrt(HDIM)

    def first(self):
        return pl.BlockSpec((self.rows, self.cols), lambda i: (0, i))

    def second(self):
        return pl.BlockSpec((self.rows, self.cols), lambda i: (0, self.steps + i))

    def memory(self, part):
        slots = self.memory_rows // (CAP * BLK)
        return pl.BlockSpec(
            (slots, 2, CAP * BLK, self.cols), lambda i: (0, 0, 0, part * self.steps + i)
        )

    def pair(self):
        return pl.BlockSpec((2 * self.rows, self.cols), lambda i: (0, i))

    def whole(self, shape):
        return pl.BlockSpec(shape, lambda i: (0,) * len(shape))

    def stacked(self):
        return pl.BlockSpec((2, self.rows, self.cols), lambda i: (0, 0, i))


def joined(refs, lanes):
    return jnp.concatenate([ref[:, lanes] for ref in refs], axis=0)


def scores_of(plan, query, key_refs, memory_ref, bias, memory_bias_ref, lanes, rows):
    scaling = plan.scale * LOG2E
    keys = joined(key_refs, lanes)
    current = dot_nt(query, keys) * scaling + bias
    parts, memory_keys = [], []
    for part in range(2):
        mem = memory_ref[:, part, :, lanes].reshape(plan.memory_rows, HDIM)
        score = dot_nt(query[part * rows : (part + 1) * rows], mem)
        parts.append(score * scaling + memory_bias_ref[part : part + 1, :])
        memory_keys.append(mem)
    return keys, memory_keys, current, jnp.concatenate(parts, axis=0)


def widened(column, like):
    return jnp.concatenate([column] * (like.shape[1] // column.shape[1]), axis=1)


def attend_near(plan, own_qd, far_qd, kv, memory, key_row, query_col, memory_bias, token):
    rows = plan.rows

    def body(qo, qf, k0, k1, v0, v1, mk, mv, krow, qcol, mbias, _, mixed_out, top_out, total_out):
        bias = visible_bias(krow[0:1, :], krow[1:2, :], qcol[:, 0:1], qcol[:, 1:2])
        for g in range(plan.group):
            lanes = slice(g * HDIM, (g + 1) * HDIM)
            query = joined((qo, qf), lanes)
            _, _, current, mem = scores_of(plan, query, (k0, k1), mk, bias, mbias, lanes, rows)
            top = jnp.maximum(
                jnp.max(current, axis=1, keepdims=True), jnp.max(mem, axis=1, keepdims=True)
            )
            weight = jnp.exp2(current - top)
            mem_weight = jnp.exp2(mem - top)
            total = jnp.sum(weight, axis=1, keepdims=True) + jnp.sum(
                mem_weight, axis=1, keepdims=True
            )
            mixed = dot_nn(weight.astype(BF16), joined((v0, v1), lanes))
            mem16 = mem_weight.astype(BF16)
            mixed_mem = [
                dot_nn(
                    mem16[part * rows : (part + 1) * rows],
                    mv[:, part, :, lanes].reshape(plan.memory_rows, HDIM),
                )
                for part in range(2)
            ]
            mixed_out[:, lanes] = mixed + jnp.concatenate(mixed_mem, axis=0)
            top_out[:, lanes] = jnp.broadcast_to(top, (2 * rows, HDIM))
            total_out[:, lanes] = jnp.broadcast_to(total, (2 * rows, HDIM))

    flops = 2 * 2 * (2 * rows) * (2 * rows + plan.memory_rows) * plan.half
    return pl.pallas_call(
        body,
        grid=(plan.steps,),
        out_shape=(jax.ShapeDtypeStruct((2 * rows, plan.half), F32),) * 3,
        in_specs=[plan.first()] * 4
        + [plan.second()] * 2
        + [plan.memory(0), plan.memory(1)]
        + [plan.whole(key_row.shape), plan.whole(query_col.shape), plan.whole(memory_bias.shape)]
        + [plan.whole(token.shape)],
        out_specs=(plan.pair(),) * 3,
        cost_estimate=cost(flops, 12 * rows * plan.half * 2, 2 * rows * 3 * rows * plan.heads),
        compiler_params=pltpu.CompilerParams(vmem_limit_bytes=VMEM_BYTES),
        name="attend_near",
    )(own_qd, far_qd, *kv, *kv, memory, memory, key_row, query_col, memory_bias, token)


def attend_prev(plan, own_qd, far_qd, kv, key_row, query_col, near):
    rows = plan.rows

    def body(
        qo, qf, do_o, do_f, k0, k1, v0, v1, krow, qcol, mixed_in, top_in, total_in,
        att_own, att_far, level_out, delta_out, stat_row,
    ):
        bias = visible_bias(krow[0:1, :], krow[1:2, :], qcol[:, 0:1], qcol[:, 1:2])
        lane = lax.broadcasted_iota(jnp.int32, (2 * rows, HDIM), 1)
        stats = jnp.zeros((2 * rows, HDIM), F32)
        scaling = plan.scale * LOG2E
        for g in range(plan.group):
            lanes = slice(g * HDIM, (g + 1) * HDIM)
            query = joined((qo, qf), lanes)
            score = dot_nt(query, joined((k0, k1), lanes)) * scaling + bias
            near_top = top_in[:, lanes]
            top = jnp.maximum(
                jnp.broadcast_to(jnp.max(score, axis=1, keepdims=True), near_top.shape), near_top
            )
            weight = jnp.exp2(score - widened(top, score))
            shrink = jnp.exp2(near_top - top)
            total = jnp.sum(weight, axis=1, keepdims=True) + total_in[:, lanes] * shrink
            mixed = dot_nn(weight.astype(BF16), joined((v0, v1), lanes))
            output = (mixed + mixed_in[:, lanes] * shrink) / total
            upstream = joined((do_o, do_f), lanes).astype(F32)
            delta = jnp.sum(upstream * output, axis=1, keepdims=True)
            level = top + jnp.log2(total)
            stats = jnp.where(lane == g, level, stats)
            stats = jnp.where(lane == plan.group + g, delta, stats)
            level_out[:, lanes] = level
            delta_out[:, lanes] = jnp.broadcast_to(delta, level.shape)
            att_own[:, lanes] = output[:rows].astype(BF16)
            att_far[:, lanes] = output[rows:].astype(BF16)
        stat_row[0] = stats.T[0:8, :]

    flops = 2 * 2 * (2 * rows) * (2 * rows) * plan.half
    return pl.pallas_call(
        body,
        grid=(plan.steps,),
        out_shape=(
            jax.ShapeDtypeStruct((rows, plan.half), BF16),
            jax.ShapeDtypeStruct((rows, plan.half), BF16),
            jax.ShapeDtypeStruct((2 * rows, plan.half), F32),
            jax.ShapeDtypeStruct((2 * rows, plan.half), F32),
            jax.ShapeDtypeStruct((plan.steps, 8, 2 * rows), F32),
        ),
        in_specs=[plan.first()] * 2
        + [plan.second()] * 2
        + [plan.first()] * 2
        + [plan.second()] * 2
        + [plan.whole(key_row.shape), plan.whole(query_col.shape)]
        + [plan.pair()] * 3,
        out_specs=(
            plan.first(),
            plan.first(),
            plan.pair(),
            plan.pair(),
            pl.BlockSpec((1, 8, 2 * rows), lambda i: (i, 0, 0)),
        ),
        cost_estimate=cost(flops, 16 * rows * plan.half * 2, 4 * rows * rows * plan.heads),
        compiler_params=pltpu.CompilerParams(vmem_limit_bytes=VMEM_BYTES),
        name="attend_prev",
    )(
        own_qd, far_qd, own_qd, far_qd, *kv, *kv, key_row, query_col, *near
    )


def query_gradients(plan, own_qd, far_qd, kv, memory, key_row, query_col, memory_bias, level, delta):
    rows = plan.rows

    def body(
        qo, qf, do_o, do_f, k0, k1, k2, k3, v0, v1, v2, v3, mk, mv, krow, qcol, mbias,
        level_in, delta_in, dq_own, dq_far, squares,
    ):
        bias = visible_bias(krow[0:1, :], krow[1:2, :], qcol[:, 0:1], qcol[:, 1:2])
        acc = jnp.zeros((8, HDIM), F32)
        for g in range(plan.group):
            lanes = slice(g * HDIM, (g + 1) * HDIM)
            query = joined((qo, qf), lanes)
            upstream = joined((do_o, do_f), lanes)
            level = level_in[:, lanes]
            delta = delta_in[:, lanes]
            keys, mem_keys, current, mem = scores_of(
                plan, query, (k0, k1, k2, k3), mk, bias, mbias, lanes, rows
            )
            values = joined((v0, v1, v2, v3), lanes)
            press = dot_nt(upstream, values) - widened(delta, current)
            prob = jnp.exp2(current - widened(level, current))
            grad = (prob * press).astype(BF16)
            result = dot_nn(grad, keys)
            extra = []
            for part in range(2):
                span = slice(part * rows, (part + 1) * rows)
                mem_values = mv[:, part, :, lanes].reshape(plan.memory_rows, HDIM)
                mem_press = dot_nt(upstream[span], mem_values) - widened(delta[span], mem)
                mem_grad = (jnp.exp2(mem[span] - widened(level[span], mem)) * mem_press).astype(BF16)
                extra.append(dot_nn(mem_grad, mem_keys[part]))
            result = (result + jnp.concatenate(extra, axis=0)) * plan.scale
            dq_own[:, lanes] = result[:rows]
            dq_far[:, lanes] = result[rows:].astype(BF16)
            acc = acc + jnp.sum((result * result).reshape(-1, 8, HDIM), axis=0)

        @pl.when(pl.program_id(0) == 0)
        def _():
            squares[...] = jnp.zeros_like(squares)

        squares[...] += acc

    flops = 3 * (4 * rows + plan.memory_rows) * 2 * (2 * rows) * plan.half
    return pl.pallas_call(
        body,
        grid=(plan.steps,),
        out_shape=(
            pltpu.HBM((rows, plan.half), F32),
            jax.ShapeDtypeStruct((rows, plan.half), BF16),
            jax.ShapeDtypeStruct((8, HDIM), F32),
        ),
        in_specs=[plan.first()] * 2
        + [plan.second()] * 2
        + [plan.first()] * 4
        + [plan.second()] * 4
        + [plan.memory(0), plan.memory(1)]
        + [plan.whole(key_row.shape), plan.whole(query_col.shape), plan.whole(memory_bias.shape)]
        + [plan.pair()] * 2,
        out_specs=(plan.first(), plan.first(), plan.whole((8, HDIM))),
        cost_estimate=cost(flops, 14 * rows * plan.half * 2, 2 * rows * 5 * rows * plan.heads),
        compiler_params=pltpu.CompilerParams(vmem_limit_bytes=VMEM_BYTES),
        name="query_gradients",
    )(
        own_qd, far_qd, own_qd, far_qd, *kv, *kv, memory, memory, key_row, query_col, memory_bias,
        level, delta,
    )


def key_terms(plan, key, value, query, upstream, bias, level, delta):
    score = dot_nt(key, query) * (plan.scale * LOG2E) + bias
    prob = jnp.exp2(score - level)
    grad = (prob * (dot_nt(value, upstream) - delta)).astype(BF16)
    return dot_nn(grad, query) * plan.scale, dot_nn(prob.astype(BF16), upstream)


def key_gradients(plan, qd, own_kv, far_kv, query_row, key_col, near_stats, next_stats, dq_squares, devices):
    rows = plan.rows

    def body(
        q0, q1, q2, q3, do0, do1, do2, do3, k0, k1, v0, v1, qrow, kcol, stat0, stat1, dq_sq,
        dk_own, dv_own, send, share, squares,
    ):
        bias = visible_bias(kcol[:, 0:1], kcol[:, 1:2], qrow[0:1, :], qrow[1:2, :])
        acc = jnp.zeros((8, HDIM), F32)
        for g in range(plan.group):
            lanes = slice(g * HDIM, (g + 1) * HDIM)
            key_part, value_part = key_terms(
                plan,
                joined((k0, k1), lanes),
                joined((v0, v1), lanes),
                joined((q0, q1, q2, q3), lanes),
                joined((do0, do1, do2, do3), lanes),
                bias,
                *[
                    jnp.concatenate([stat0[0, n : n + 1, :], stat1[0, n : n + 1, :]], axis=1)
                    for n in (g, plan.group + g)
                ],
            )
            dk_own[:, lanes] = key_part[:rows]
            dv_own[:, lanes] = value_part[:rows]
            send[0, :, lanes] = key_part[rows:].astype(BF16)
            send[1, :, lanes] = value_part[rows:].astype(BF16)
            both = key_part * key_part + value_part * value_part
            acc = acc + jnp.sum(both.reshape(-1, 8, HDIM), axis=0)

        @pl.when(pl.program_id(0) == 0)
        def _():
            squares[...] = dq_sq[...]

        squares[...] += acc

        @pl.when(pl.program_id(0) == plan.steps - 1)
        def _():
            row = jnp.sum(squares[...], axis=0, keepdims=True)
            share[...] = jnp.broadcast_to(row, share.shape)

    stat = pl.BlockSpec((1, 8, 2 * rows), lambda i: (i, 0, 0))
    return pl.pallas_call(
        body,
        grid=(plan.steps,),
        out_shape=(
            jax.ShapeDtypeStruct((rows, plan.half), F32),
            jax.ShapeDtypeStruct((rows, plan.half), F32),
            pltpu.HBM((2, rows, plan.half), BF16),
            pltpu.HBM((devices, HDIM), F32),
        ),
        in_specs=[plan.first()] * 4
        + [plan.second()] * 4
        + [plan.first()] * 2
        + [plan.second()] * 2
        + [plan.whole(query_row.shape), plan.whole(key_col.shape)]
        + [stat, stat, plan.whole((8, HDIM))],
        out_specs=(plan.first(), plan.first(), plan.stacked(), plan.whole((devices, HDIM))),
        scratch_shapes=[pltpu.VMEM((8, HDIM), F32)],
        cost_estimate=cost(
            2 * 4 * 2 * (2 * rows) ** 2 * plan.half, 24 * rows * plan.half * 2, 8 * rows * rows * plan.heads
        ),
        compiler_params=pltpu.CompilerParams(vmem_limit_bytes=VMEM_BYTES),
        name="key_gradients",
    )(
        *qd, *qd, own_kv, far_kv, own_kv, far_kv, query_row, key_col, near_stats, next_stats, dq_squares,
    )


def scaled(plan, side, shares, entries, dq_own, dq_far, dk_own, dv_own, kv_far):
    rows, half = plan.rows, plan.half

    def body(side_ref, share, dq, dq_other, dk, dv, other, dq_out, dk_out, dv_out):
        squares = jnp.sum(jnp.sum(share[...], axis=0, keepdims=True), axis=1, keepdims=True)
        inverse = 1.0 / jnp.sqrt(squares / entries + 1e-06)
        near = pl.multiple_of(side_ref[0] * half, half)
        away = pl.multiple_of(half - side_ref[0] * half, half)
        for out, mine, theirs in (
            (dq_out, dq[...], dq_other[...]),
            (dk_out, dk[...], other[0]),
            (dv_out, dv[...], other[1]),
        ):
            out[:, pl.ds(near, half)] = (mine * inverse).astype(BF16)
            out[:, pl.ds(away, half)] = (theirs.astype(F32) * inverse).astype(BF16)

    vmem = pl.BlockSpec(memory_space=pltpu.VMEM)
    return pl.pallas_call(
        body,
        out_shape=(jax.ShapeDtypeStruct((rows, 2 * half), BF16),) * 3,
        in_specs=[pl.BlockSpec(memory_space=pltpu.SMEM)] + [vmem] * 6,
        out_specs=(vmem,) * 3,
        cost_estimate=cost(6 * rows * half, 20 * rows * half),
        compiler_params=pltpu.CompilerParams(vmem_limit_bytes=VMEM_BYTES),
        name="scaled",
    )(side, shares, dq_own, dq_far, dk_own, dv_own, kv_far)


def on_device(query, keys, values, memory_keys, memory_values, routes, documents, cotangent):
    rows, width = query.shape
    half = width // 2
    count = lax.axis_size("ctx")
    devices = count * lax.axis_size("head")
    position = lax.axis_index("ctx").astype(jnp.int32)
    side = position % 2
    partner = position + 1 - 2 * side
    per_device = memory_keys.shape[0] // BLK
    memory_rows = count * CAP * BLK
    plan = Plan(rows, half, memory_rows)

    packed = pack_memory(position, routes, memory_keys, memory_values, count)
    own_kv, sent_kv = halves(position, keys, values)
    own_qd, sent_qd = halves(position, query, cotangent)
    far_kv = swapped(sent_kv)
    prev_own_kv = shifted(own_kv, 2)
    next_own_qd = shifted(own_qd, -2)
    token = prev_own_kv[:8, :128] + far_kv[:8, :128]
    for _ in range(6):
        token = lax.ppermute(token, "head", [(i, i ^ 1) for i in range(lax.axis_size("head"))])
    far_kv, sent_qd = lax.optimization_barrier((far_kv, sent_qd))
    relayed_kv, token = lax.optimization_barrier((far_kv, token))
    prev_far_kv = shifted(relayed_kv, 2)
    far_qd = swapped(sent_qd)
    route_table = routes[:, 0].reshape(count, per_device)
    arrived = lax.all_to_all(
        packed.reshape(count, 2 * CAP * BLK, width), "ctx", split_axis=0, concat_axis=0, tiled=True
    ).reshape(count, 2, CAP * BLK, width)

    def labels(block):
        docs = lax.dynamic_slice_in_dim(documents, block * rows, rows)
        docs = jnp.where((block >= 0) & (block < count), docs, -1)
        return jnp.stack([docs, block * rows + jnp.arange(rows, dtype=jnp.int32)])

    near_row = jnp.concatenate([labels(position), labels(partner)], axis=1)
    prev_row = jnp.concatenate([labels(position - 2), labels(partner - 2)], axis=1)
    next_row = jnp.concatenate([labels(position + 2), labels(partner + 2)], axis=1)
    key_row = jnp.concatenate([near_row, prev_row], axis=1)
    near_col = near_row.T
    readers = jnp.stack([position, partner])
    arrivals = jnp.sum((route_table[None] == readers[:, None, None]).astype(jnp.int32), axis=2)
    live = jnp.arange(CAP, dtype=jnp.int32)[None, None, :] < arrivals[:, :, None]
    memory_bias = jnp.broadcast_to(
        jnp.where(live, 0.0, NEGATIVE)[..., None], (2, count, CAP, BLK)
    ).reshape(2, memory_rows)

    query_row = jnp.concatenate([near_row, next_row], axis=1)
    far_qd, near_row, prev_row, query_row, key_row, near_col, memory_bias = lax.optimization_barrier(
        (far_qd, near_row, prev_row, query_row, key_row, near_col, memory_bias)
    )
    next_far_qd = shifted(far_qd, -2)
    kv = (own_kv, far_kv, prev_own_kv, prev_far_kv)
    near = attend_near(plan, own_qd, far_qd, kv[:2], arrived, near_row, near_col, memory_bias, token)
    att_own, att_far, level, delta, stat_row = attend_prev(
        plan, own_qd, far_qd, kv[2:], prev_row, near_col, near
    )
    next_stats = shifted(stat_row, -2)
    att_back = swapped(att_far)
    dq_own, dq_far, dq_squares = query_gradients(
        plan, own_qd, far_qd, kv, arrived, key_row, near_col, memory_bias, level, delta
    )
    next_stats, dq_far, att_back = lax.optimization_barrier((next_stats, dq_far, att_back))
    dq_back = swapped(dq_far)
    dk_own, dv_own, second_send, share = key_gradients(
        plan, (own_qd, far_qd, next_own_qd, next_far_qd), own_kv, far_kv, query_row, near_col,
        stat_row, next_stats, dq_squares, devices,
    )
    second_send, dq_back = lax.optimization_barrier((second_send, dq_back))
    second_back = swapped(second_send)
    shares = lax.all_to_all(share, ("ctx", "head"), split_axis=0, concat_axis=0, tiled=True)
    entries = 3.0 * count * rows * width * lax.axis_size("head")
    query_grad, key_grad, value_grad = scaled(
        plan, side[None], shares, entries, dq_own, dq_back, dk_own, dv_own, second_back
    )
    attended = jnp.where(
        side == 0,
        jnp.concatenate([att_own, att_back], axis=1),
        jnp.concatenate([att_back, att_own], axis=1),
    )
    return attended, query_grad, key_grad, value_grad


def solution(mesh):
    spread = P("ctx", "head")
    return jax.shard_map(
        on_device,
        mesh=mesh,
        in_specs=(spread,) * 5 + (P(), P(), spread),
        out_specs=(spread,) * 4,
        check_vma=False,
    )
```
